256 devices in a mesh: rep: 64 (over z, y, core), shard: 4 (over x).
Axes of the slice: x: 4, y: 4, z: 8, core: 2. Of those that a mesh axis runs over, the one named last changes fastest.
Arguments:
- q_grad: float32 [64, 1152, 1152], P('rep', None, 'shard'), may hold values from -16 to 16
- o_grad: float32 [64, 1152, 1152], P('rep', None, 'shard'), may hold values from -16 to 16
- q_error: float32 [64, 1152, 1152], P('rep', None, 'shard'), may hold values from -4 to 4
- o_error: float32 [64, 1152, 1152], P('rep', None, 'shard'), may hold values from -4 to 4
- q_basis: float32 [1152, 32], P('shard'), may hold values from -6 to 6
- o_basis: float32 [1152, 32], P('shard'), may hold values from -6 to 6
- q_moment: float32 [1152, 1152], P('rep', 'shard'), may hold values from -6 to 6
- o_moment: float32 [1152, 1152], P('rep', 'shard'), may hold values from -6 to 6
- q_weight: float32 [1152, 1152], P('rep', 'shard'), may hold values from -0.1875 to 0.1875
- o_weight: float32 [1152, 1152], P('rep', 'shard'), may hold values from -0.1875 to 0.1875
- norm_grads: float32 [64, 4, 2304], P('rep', 'shard'), may hold values from -6 to 6
- norm_moment: float32 [2304], P(('rep', 'shard')), may hold values from -6 to 6
- norm_weight: float32 [2304], P(('rep', 'shard')), may hold values from 0.5 to 1.5
Outputs:
- q_weight_new: float32 [1152, 1152], P(None, 'shard')
- o_weight_new: float32 [1152, 1152], P(None, 'shard')
- q_moment_new: float32 [1152, 1152], P('rep', 'shard')
- o_moment_new: float32 [1152, 1152], P('rep', 'shard')
- q_error_new: float32 [64, 1152, 1152], P('rep', None, 'shard')
- o_error_new: float32 [64, 1152, 1152], P('rep', None, 'shard')
- norm_weight_new: float32 [2304], replicated
- norm_moment_new: float32 [2304], P(('rep', 'shard'))
The draws below stay inside these ranges and needn't reach their ends.
All inputs are finite; a program needn't handle non-finite values.
Results may differ from the reference program's by a relative error of at most 0.0003.
Values sent between devices are 32-bit elements; how exact they have to be, the bound alone decides.
A program may use at most 64 MiB of HBM per device.

```python
import jax
import jax.numpy as jnp
from jax import lax

D = 1152
RANK = 32
ROUNDS = 2
FLAT = 2304
N_REP = 64
N_SHARD = 4


def spiked(result, stream_key, source, target, parts, factor):
    def block_of(position):
        return (jnp.arange(result.shape[position]) // (result.shape[position] // parts)).reshape((-1,) + (1,) * (result.ndim - 1 - position))

    first = jax.random.permutation(stream_key, parts)[block_of(target)]
    other_side = (block_of(target) + parts // 2) % parts
    return jnp.where((block_of(source) == first) | (block_of(source) == other_side), factor * result, result)


def block_levels(stream_key, shape, cuts, smallest, high):
    factor_of, own = 1.0, jax.random.fold_in(stream_key, 6)
    for position, shards_of in cuts:
        heights = jnp.exp(jax.random.uniform(jax.random.fold_in(own, position), (shards_of,), jnp.float32, smallest / len(cuts), high / len(cuts)))
        factor_of = factor_of * jnp.repeat(heights, shape[position] // shards_of).reshape([-1 if axis == position else 1 for axis in range(len(shape))])
    return factor_of


def scatter_about(rng, shape, scale, most, split=(), held_as=jnp.bfloat16):
    result = jax.random.normal(rng, shape, jnp.float32) * scale
    if len(split) > 0:
        result = block_levels(rng, shape, split, -0.22, 0.18) * result
    return jnp.clip(result, min=-most, max=most).astype(held_as)


def gaussian_with(key, extent, spread, reach, cuts, heavy, dtype=jnp.bfloat16):
    drawn = spread * jax.random.normal(key, extent, jnp.float32)
    if cuts:
        drawn = drawn * block_levels(key, extent, cuts, -0.22, 0.18)
    return jnp.clip(spiked(drawn, jax.random.fold_in(key, 3), *heavy), -reach, reach).astype(dtype)


def setup_inputs(seed: int = 0) -> dict:
    keys = jax.random.split(jax.random.key(seed), 14)
    q_grad = gaussian_with(keys[0], (N_REP, D, D), 1.0, 16.0, ((0, 64), (2, 4)), (0, 1, 64, 4.0), jnp.float32)
    o_grad = gaussian_with(keys[1], (N_REP, D, D), 1.0, 16.0, ((0, 64), (2, 4)), (0, 1, 64, 4.0), jnp.float32)
    q_error = scatter_about(keys[2], (N_REP, D, D), 0.5, 4.0, ((0, 64), (2, 4)), jnp.float32)
    o_error = scatter_about(keys[3], (N_REP, D, D), 0.5, 4.0, ((0, 64), (2, 4)), jnp.float32)
    q_basis = scatter_about(keys[4], (D, RANK), 1.0, 6.0, ((0, 4),), jnp.float32)
    o_basis = scatter_about(keys[5], (D, RANK), 1.0, 6.0, ((0, 4),), jnp.float32)
    q_moment = scatter_about(keys[6], (D, D), 1.0, 6.0, ((0, 64), (1, 4)), jnp.float32)
    o_moment = scatter_about(keys[7], (D, D), 1.0, 6.0, ((0, 64), (1, 4)), jnp.float32)
    q_weight = scatter_about(keys[8], (D, D), D ** -0.5, 0.1875, ((0, 64), (1, 4)), jnp.float32)
    o_weight = scatter_about(keys[9], (D, D), D ** -0.5, 0.1875, ((0, 64), (1, 4)), jnp.float32)
    norm_grads = gaussian_with(keys[10], (N_REP, N_SHARD, FLAT), 0.25, 6.0, ((0, 64), (1, 4)), (0, 2, 64, 4.0), jnp.float32)
    norm_moment = scatter_about(keys[11], (FLAT,), 1.0, 6.0, ((0, 256),), jnp.float32)
    norm_weight = jnp.clip(1.0 + 0.1 * jax.random.normal(keys[12], (FLAT,), jnp.float32), 0.5, 1.5)
    return dict(q_grad=q_grad, o_grad=o_grad, q_error=q_error, o_error=o_error, q_basis=q_basis, o_basis=o_basis, q_moment=q_moment, o_moment=o_moment, q_weight=q_weight, o_weight=o_weight, norm_grads=norm_grads, norm_moment=norm_moment, norm_weight=norm_weight)


highest = lax.Precision.HIGHEST
decay_rate = 0.9
step_size = 0.1

def unwhiten(lower, factor):
    return jax.scipy.linalg.solve_triangular(lower, factor.T, lower=True).T

def compress(grad, error, basis):
    corrected = grad + error
    total = jnp.sum(corrected, axis=0)
    normal = None
    for sweep in range(ROUNDS):
        left = jnp.dot(total, basis, precision=highest)
        gram = jnp.dot(left.T, left, precision=highest)
        lower = jnp.linalg.cholesky(gram)
        normal = unwhiten(lower, left)
        basis = jnp.dot(total.T, normal, precision=highest)
    decoded = jnp.dot(normal, basis.T, precision=highest)
    return (corrected - decoded[None], decoded)

def reference(q_grad, o_grad, q_error, o_error, q_basis, o_basis, q_moment, o_moment, q_weight, o_weight, norm_grads, norm_moment, norm_weight):
    q_error_new, q_decoded = compress(q_grad, q_error, q_basis)
    o_error_new, o_decoded = compress(o_grad, o_error, o_basis)
    q_moment_new = decay_rate * q_moment + q_decoded
    o_moment_new = decay_rate * o_moment + o_decoded
    q_weight_new = q_weight - step_size * q_moment_new
    o_weight_new = o_weight - step_size * o_moment_new
    norm_sum = jnp.sum(norm_grads, axis=(0, 1))
    norm_moment_new = decay_rate * norm_moment + norm_sum
    norm_weight_new = norm_weight - step_size * norm_moment_new
    return (q_weight_new, o_weight_new, q_moment_new, o_moment_new, q_error_new, o_error_new, norm_weight_new, norm_moment_new)
```

```python
import functools

import jax
import jax.numpy as jnp
from jax import lax
from jax.experimental import pallas as pl
from jax.experimental.pallas import tpu as pltpu
from jax.sharding import PartitionSpec as P

MESH = pl.DeviceIdType.MESH
F32 = jnp.float32
BF16 = jnp.bfloat16
HI = lax.Precision.HIGHEST
DECAY = 0.9
STEP = 0.1
NZ, NY, NX = 8, 4, 4
STARTS = [2 * z + (z + 7) // 8 + (z + 3) // 8 for z in range(NZ)]
COUNTS = [24 if z % 4 == 0 else 16 for z in range(NZ)]


def dot(a, b, ca, cb):
    return lax.dot_general(a, b, (((ca,), (cb,)), ((), ())), precision=HI, preferred_element_type=F32)


def iota(shape, axis):
    return lax.broadcasted_iota(jnp.int32, shape, axis)


def parts_of(value):
    one = value.astype(BF16).astype(F32)
    two = (value - one).astype(BF16).astype(F32)
    three = (value - one - two).astype(BF16).astype(F32)
    return one, two, three


def rows_of(z):
    return pl.multiple_of(8 * (2 * z + (z + 7) // 8 + (z + 3) // 8), 8)


def inverse_factor(gram):
    lane, row = iota((32, 128), 1), iota((32, 128), 0)
    is_q = (lane // 32) % 2 == 0
    is_q1 = is_q[:1]
    eye = jnp.where((lane >= 64) & (lane % 32 == row), 1.0, 0.0).astype(F32)
    work = jnp.concatenate([gram, eye[:, 64:]], axis=1)
    for k in range(32):
        pivot_row = work[k : k + 1]
        pivot = jnp.where(is_q1, pivot_row[:, k : k + 1], pivot_row[:, 32 + k : 33 + k])
        column = jnp.where(is_q, work[:, k : k + 1], work[:, 32 + k : 33 + k])
        work = work - jnp.where(row > k, column, 0.0) * (pivot_row / pivot)
    dq = jnp.sum(jnp.where(lane == row, work, 0.0), axis=1, keepdims=True)
    do = jnp.sum(jnp.where(lane == row + 32, work, 0.0), axis=1, keepdims=True)
    scale = 1.0 / jnp.sqrt(jnp.where(is_q, dq, do))
    return (work * scale)[:, 64:]


def block_diagonal(pair):
    lane = iota((32, 64), 1)
    return jnp.concatenate([jnp.where(lane < 32, pair, 0.0), jnp.where(lane >= 32, pair, 0.0)], axis=0)


def communicate(
    qg, og, qe, oe, qb, ob, qm, om, qw, ow, ng, nm, nw,
    corr_q, corr_o, ut_q, ut_o, lstack, p_out, own_left, norm_out,
    err, qbv, obv, qmv, omv, qwv, owv, ngv, nmv, nwv, full, rcv, ya, yb, yc, yd, zbuf, zrecv, tpack, e0,
    nx, upk, ug, ub, uall, lx, rsend, rrecv, rz, rag, rt, lgz, lfold, lsc, l2,
    in_sem, sm_sem, s_core, r_core, s_y, r_y, s_z, r_z, s_nx, r_nx, s_u, r_u, s_ur, r_ur, s_uc, r_uc, u_loc,
    s_lx, r_lx, s_rg, r_rg, s_rz, r_rz, s_ra, r_ra, s_lz, r_lz, s_lg, r_lg,
):
    r = lax.axis_index("rep")
    s = lax.axis_index("shard")
    z, g = r // 8, r % 8
    y, c = g // 2, g % 2
    partner = r + 1 - 2 * c
    sends = []

    def rep_of(zz, yy, cc):
        return zz * 8 + yy * 2 + cc

    def copy(src, dst, ssem, rsem, rep, shard):
        d = pltpu.make_async_remote_copy(src_ref=src, dst_ref=dst, send_sem=ssem, recv_sem=rsem, device_id=(rep, shard), device_id_type=MESH)
        d.start()
        sends.append(d)
        return d

    def over_g(k):
        return z * 8 + (g + k) % 8

    def over_z(k):
        return ((z + k) % NZ) * 8 + g

    def over_x(k):
        return (s + k) % NX

    def load(src, dst, sem):
        d = pltpu.make_async_copy(src, dst, sem)
        d.start()
        return d

    small = [
        load(src, dst, sm_sem.at[i])
        for i, (src, dst) in enumerate(
            ((qb, qbv), (ob, obv), (qm, qmv), (om, omv), (qw, qwv), (ow, owv), (ng, ngv), (nm, nmv), (nw, nwv))
        )
    ]
    cuts = ((0, pl.ds(0, 128)), (0, pl.ds(128, 128)), (1, pl.ds(0, 128)), (1, pl.ds(128, 128)), (0, pl.ds(256, 32)), (1, pl.ds(256, 32)))
    loads = []
    for i, (p, cut) in enumerate(cuts):
        grad, error, corr = ((qg, qe, corr_q), (og, oe, corr_o))[p]
        loads.append((load(grad.at[cut], corr.at[cut], in_sem.at[0, i]), load(error.at[cut], err.at[p, cut], in_sem.at[1, i])))

    barrier = pltpu.get_barrier_semaphore()
    for k in range(1, 8):
        pl.semaphore_signal(barrier, inc=1, device_id=(over_g(k), s), device_id_type=MESH)
        pl.semaphore_signal(barrier, inc=1, device_id=(over_z(k), s), device_id_type=MESH)
    for k in range(1, 4):
        pl.semaphore_signal(barrier, inc=1, device_id=(r, over_x(k)), device_id_type=MESH)

    for d in small:
        d.wait()
    uq = qwv[...] - (STEP * DECAY) * qmv[...]
    uo = owv[...] - (STEP * DECAY) * omv[...]
    upk[...] = jnp.zeros_like(upk)
    upk[0:18, 0:256] = uq[:, 0:256]
    upk[0:18, 256:512] = uo[:, 0:256]
    upk[0:18, 512:576] = jnp.concatenate([uq[:, 256:288], uo[:, 256:288]], axis=1)
    flat = iota((24, 128), 0) * 128 + iota((24, 128), 1) - 9 * (r * 4 + s)
    gains = jnp.zeros((24, 128), F32)
    for k in range(9):
        gains = jnp.where(flat == k, nwv[k] - (STEP * DECAY) * nmv[k], gains)
    nx[s, 16:24, :] = jnp.zeros((8, 128), F32)
    for i in range(18):
        nx[s, i : i + 1, :] = ngv[0, :, 128 * i : 128 * i + 128]
    nx[s, 24:48, :] = gains
    e0[...] = jnp.zeros_like(e0)
    e0[0:32, 0:256] = qbv[:, 0:256]
    e0[0:32, 512:544] = qbv[:, 256:288]
    e0[32:64, 256:512] = obv[:, 0:256]
    e0[32:64, 544:576] = obv[:, 256:288]
    zbuf[:, 144:152, :] = jnp.zeros((5, 8, 128), F32)

    pl.semaphore_wait(barrier, 17)

    norm_copies = [copy(nx.at[s], nx.at[s], s_nx.at[k - 1], r_nx.at[k - 1], r, over_x(k)) for k in range(1, 4)]
    u_core = y // 2
    u_copies = []
    for k in range(1, 4):
        u_copies.append(copy(upk, ug.at[g % 4], s_u.at[k], r_u.at[g % 4], rep_of(z, (y + k) % 4, u_core), s))
    u_local = pltpu.make_async_copy(upk, ug.at[g % 4], r_u.at[g % 4])
    u_cross = pltpu.make_async_remote_copy(
        src_ref=upk, dst_ref=ug.at[g % 4], send_sem=s_u.at[0], recv_sem=r_u.at[g % 4], device_id=(partner, s), device_id_type=MESH
    )

    def add_in(i):
        for d in loads[i]:
            d.wait()
        p, cut = cuts[i]
        corr = (corr_q, corr_o)[p]
        corr[cut, :] = corr[cut, :] + err[p, cut, :]

    core_copies = []
    here, there = pl.multiple_of(c * 576, 576), pl.multiple_of((1 - c) * 576, 576)
    for j in range(5):
        if j < 4:
            add_in(j)
        else:
            add_in(4)
            add_in(5)
        for t in range(9):
            lanes = slice(128 * t, 128 * t + 128)
            if j < 4:
                block = (corr_q, corr_o)[j // 2][128 * (j % 2) : 128 * (j % 2) + 128, lanes]
            else:
                block = jnp.concatenate([corr_q[256:288, lanes], corr_o[256:288, lanes], jnp.zeros((64, 128), F32)], axis=0)
            full[j, lanes, :] = block.T
        core_copies.append(copy(full.at[j, pl.ds(there, 576), :], rcv.at[j], s_core.at[j], r_core.at[j], partner, s))

    up, down = rep_of(z, (y + 1) % 4, c), rep_of(z, (y + 3) % 4, c)
    y_plus, y_two, y_minus = (y + 1) % 4, (y + 2) % 4, (y + 3) % 4
    y_first, y_plain, y_second, z_copies = {}, {}, {}, {}

    def half_of(yy, part):
        return pl.ds(pl.multiple_of(c * 576 + yy * 144 + part * 72, 8), 72)

    def stage_core(j):
        core_copies[j].wait_recv()

        def body(t, carry):
            rows = pl.ds(pl.multiple_of(here + t * 72, 8), 72)
            full[j, rows, :] = full[j, rows, :] + rcv[j, pl.ds(pl.multiple_of(t * 72, 8), 72), :]
            return carry

        lax.fori_loop(0, 8, body, 0)
        y_first[j] = [
            copy(full.at[j, half_of(y_two, 0), :], ya.at[j, 0], s_y.at[j, 0], r_y.at[j, 0], up, s),
            copy(full.at[j, half_of(y_two, 1), :], ya.at[j, 1], s_y.at[j, 1], r_y.at[j, 1], down, s),
        ]
        y_plain[j] = [
            copy(full.at[j, half_of(y_plus, 1), :], yb.at[j, 0], s_y.at[j, 2], r_y.at[j, 2], up, s),
            copy(full.at[j, half_of(y_minus, 0), :], yb.at[j, 1], s_y.at[j, 3], r_y.at[j, 3], down, s),
        ]

    def stage_relay(j):
        y_first[j][0].wait_recv()
        yc[j, 0] = full[j, half_of(y_plus, 0), :] + ya[j, 0]
        a = copy(yc.at[j, 0], yd.at[j, 0], s_y.at[j, 4], r_y.at[j, 4], up, s)
        y_first[j][1].wait_recv()
        yc[j, 1] = full[j, half_of(y_minus, 1), :] + ya[j, 1]
        b = copy(yc.at[j, 1], yd.at[j, 1], s_y.at[j, 5], r_y.at[j, 5], down, s)
        y_second[j] = [a, b]

    def stage_z(j):
        for d in y_plain[j] + y_second[j]:
            d.wait_recv()
        zbuf[j, 0:72, :] = full[j, half_of(y, 0), :] + yd[j, 0] + yb[j, 1]
        zbuf[j, 72:144, :] = full[j, half_of(y, 1), :] + yb[j, 0] + yd[j, 1]
        z_copies[j] = [
            copy(zbuf.at[j, pl.ds(rows_of((z + k) % NZ), 24), :], zrecv.at[j, k - 1], s_z.at[j, k - 1], r_z.at[j, k - 1], over_z(k), s)
            for k in (4, 3, 5, 2, 6, 1, 7)
        ]

    kept = iota((24, 128), 0) < 24 - 8 * ((z % 4 + 3) // 4)

    def stage_total(j):
        for d in z_copies[j]:
            d.wait_recv()
        value = zbuf[j, pl.ds(rows_of(z), 24), :]
        for k in range(7):
            value = value + zrecv[j, k]
        tpack[:, 128 * j : 128 * j + 128] = jnp.where(kept, value, 0.0)

    u_right, u_left, u_share, u_own = {}, {}, {}, []

    def u_at(zz, cc):
        return pl.ds(pl.multiple_of(zz * 144 + cc * 72, 8), 72)

    def u_pass(t):
        if t <= 4:
            at = (z + NZ - t + 1) % NZ
            src = ub if t == 1 else uall.at[u_at(at, c), :]
            u_right[t] = copy(src, uall.at[u_at(at, c), :], s_ur.at[0, t - 1], r_ur.at[0, t - 1], over_z(1), s)
        if t <= 3:
            at = (z + t - 1) % NZ
            src = ub if t == 1 else uall.at[u_at(at, c), :]
            u_left[t] = copy(src, uall.at[u_at(at, c), :], s_ur.at[1, t - 1], r_ur.at[1, t - 1], over_z(7), s)

    def u_begin():
        for i in range(4):
            pltpu.make_async_copy(upk, ug.at[i], r_u.at[i]).wait()
        for i in range(4):
            ub[18 * i : 18 * i + 18, :] = ug[i, 0:18, :]
        u_pass(1)
        own = pltpu.make_async_copy(ub, uall.at[u_at(z, c), :], u_loc)
        own.start()
        u_own.append(own)
        u_share[0] = copy(ub, uall.at[u_at(z, c), :], s_uc.at[0], r_uc.at[0], partner, s)

    def u_next(t):
        u_right[t - 1].wait_recv()
        if t - 1 <= 3:
            u_left[t - 1].wait_recv()
        u_pass(t)
        at = (z + NZ - (t - 1)) % NZ
        u_share[t - 1] = copy(uall.at[u_at(at, c), :], uall.at[u_at(at, c), :], s_uc.at[t - 1], r_uc.at[t - 1], partner, s)
        if t - 1 <= 3:
            at = (z + t - 1) % NZ
            u_share[t + 3] = copy(uall.at[u_at(at, c), :], uall.at[u_at(at, c), :], s_uc.at[t + 3], r_uc.at[t + 3], partner, s)

    @pl.when(u_core == c)
    def _():
        u_local.start()

    @pl.when(u_core != c)
    def _():
        u_cross.start()

    stage_core(0)
    stage_core(1)
    stage_relay(0)
    u_begin()
    stage_core(2)
    stage_relay(1)
    stage_z(0)
    stage_core(3)
    stage_relay(2)
    stage_z(1)
    stage_core(4)
    stage_relay(3)
    stage_z(2)
    stage_relay(4)
    stage_z(3)
    stage_z(4)
    for j in range(5):
        stage_total(j)

    lane = iota((32, 640), 1)
    of_q = (lane < 256) | ((lane >= 512) & (lane < 544))
    of_o = ((lane >= 256) & (lane < 512)) | ((lane >= 544) & (lane < 576))
    gram_q = (lane >= 576) & (lane < 608)

    def across(i, partial):
        lx[i, s, :, 0:64] = partial
        return [copy(lx.at[i, s], lx.at[i, s], s_lx.at[i, k - 1], r_lx.at[i, k - 1], r, over_x(k)) for k in range(1, 4)]

    def left_of(i, copies):
        for d in copies:
            d.wait_recv()
        return ((lx[i, 0] + lx[i, 1]) + (lx[i, 2] + lx[i, 3]))[:, 0:64]

    def right_begin(i, left, extra):
        tpack[:, 576:640] = left
        both = dot(left.T, tpack[...], 1, 0)
        right = jnp.where(of_q | gram_q, both[0:32], both[32:64])
        for yy in range(4):
            rsend[i, 2 * yy] = right[8 * yy : 8 * yy + 8, 0:384]
            rsend[i, 2 * yy + 1, :, 0:256] = right[8 * yy : 8 * yy + 8, 384:640]
            rsend[i, 2 * yy + 1, :, 256:384] = extra[8 * yy : 8 * yy + 8] if yy < 3 else jnp.zeros((8, 128), F32)
        copies = [
            copy(rsend.at[i, (g + k) % 8], rrecv.at[i, g], s_rg.at[i, k - 1], r_rg.at[i, k - 1], over_g(k), s) for k in (4, 5, 3, 2, 6, 7, 1)
        ]
        rrecv[i, g] = rsend[i, g]
        return copies

    def total_of(slots, i):
        return ((slots[i, 0] + slots[i, 1]) + (slots[i, 2] + slots[i, 3])) + ((slots[i, 4] + slots[i, 5]) + (slots[i, 6] + slots[i, 7]))

    def right_middle(i, copies):
        for d in copies:
            d.wait_recv()
        rz[i, z] = total_of(rrecv, i)
        return [copy(rz.at[i, z], rz.at[i, z], s_rz.at[i, k - 1], r_rz.at[i, k - 1], over_z(k), s) for k in (4, 3, 5, 2, 6, 1, 7)]

    def right_end(i, copies):
        for d in copies:
            d.wait_recv()
        rag[i, g] = total_of(rz, i)
        return [copy(rag.at[i, g], rag.at[i, g], s_ra.at[i, k - 1], r_ra.at[i, k - 1], over_g(k), s) for k in (4, 5, 3, 2, 6, 7, 1)]

    def right_read(i, copies):
        for d in copies:
            d.wait_recv()
        for yy in range(4):
            for cc in range(2):
                rt[i, 8 * yy : 8 * yy + 8, 384 * cc : 384 * cc + 384] = rag[i, 2 * yy + cc]
        return rt[i, :, 0:640]

    def spread(right):
        return jnp.concatenate([jnp.where(of_q, right, 0.0), jnp.where(of_o, right, 0.0)], axis=0)

    copies = across(0, dot(tpack[...], e0[...], 1, 1))
    u_next(2)
    for d in norm_copies:
        d.wait_recv()
    norms = (nx[0] + nx[1]) + (nx[2] + nx[3])
    left = left_of(0, copies)
    copies = right_begin(0, left, norms[0:24])
    copies = right_middle(0, copies)
    copies = right_end(0, copies)
    u_next(3)
    right = right_read(0, copies)
    copies = across(1, dot(tpack[...], spread(right), 1, 1))
    u_next(4)
    factor = block_diagonal(inverse_factor(right[:, 576:640]))
    left = dot(left_of(1, copies), factor, 1, 1)
    copies = right_begin(1, left, norms[24:48])
    lgz[z, :, 0:64] = left
    left_z = [copy(lgz.at[z], lgz.at[z], s_lz.at[k - 1], r_lz.at[k - 1], over_z(k), s) for k in (4, 3, 5, 2, 6, 1, 7)]
    copies = right_middle(1, copies)
    for d in left_z:
        d.wait_recv()
    for zz in range(NZ):
        first, count = 8 * STARTS[zz], COUNTS[zz]
        for t in range(count // 8):
            row = first + 8 * t
            value = lgz[zz, 8 * t : 8 * t + 8, 0:64]
            if row < 72:
                lfold[row : row + 8, 0:64] = value
            else:
                lfold[row - 72 : row - 64, 64:128] = value
    h = c * 4 + y
    left_g = [copy(lfold, lsc.at[h], s_lg.at[k - 1], r_lg.at[k - 1], over_g(k), s) for k in (4, 5, 3, 2, 6, 7, 1)]
    lsc[h] = lfold[...]
    copies = right_end(1, copies)
    u_right[4].wait_recv()
    at = (z + 4) % NZ
    u_share[4] = copy(uall.at[u_at(at, c), :], uall.at[u_at(at, c), :], s_uc.at[4], r_uc.at[4], partner, s)
    for d in left_g:
        d.wait_recv()
    for hh in range(8):
        l2[144 * hh : 144 * hh + 72, 0:64] = lsc[hh, :, 0:64]
        l2[144 * hh + 72 : 144 * hh + 144, 0:64] = lsc[hh, :, 64:128]
    for t in range(9):
        block = l2[128 * t : 128 * t + 128, :].T[0:64]
        one, two, three = parts_of(block)
        for p in range(2):
            rows = slice(32 * p, 32 * p + 32)
            lstack[p, :, 128 * t : 128 * t + 128] = jnp.concatenate(
                [one[rows], two[rows], one[rows], three[rows], two[rows], one[rows]], axis=0
            ).astype(BF16)
    for zz in range(8):
        for k in range(8):

            @pl.when((z == zz) & (g == k))
            def _():
                own_left[0:18, :] = l2[144 * zz + 18 * k : 144 * zz + 18 * k + 18, 0:64]

    for i in range(8):
        u_share[i].wait_recv()
    u_own[0].wait()
    for t in range(9):
        rows = slice(128 * t, 128 * t + 128)
        for j in range(4):
            (ut_q, ut_o)[j // 2][128 * (j % 2) : 128 * (j % 2) + 128, rows] = uall[rows, 128 * j : 128 * j + 128].T
        tails = uall[rows, 512:640].T
        ut_q[256:288, rows] = tails[0:32]
        ut_o[256:288, rows] = tails[32:64]
    right = right_read(1, copies)
    factor = block_diagonal(inverse_factor(right[:, 576:640]))
    p_out[...] = dot(factor, dot(factor, spread(right), 1, 0), 0, 0)
    norm_out[0] = rt[0, 0:24, 640:768]
    norm_out[1] = rt[1, 0:24, 640:768]
    for d in sends:
        d.wait_send()

    @pl.when(u_core != c)
    def _():
        u_cross.wait_send()


def decode(
    corr_q, corr_o, ut_q, ut_o, lstack, p, own_left, norms, qm, om, nm,
    qw_new, ow_new, qm_new, om_new, qe_new, oe_new, gains, nmom,
    err, weight, qmv, omv, gainv, nmv, in_sem, out_sem, sm_sem,
):
    loads = [pltpu.make_async_copy(src, dst, in_sem.at[i]) for i, (src, dst) in enumerate(((qm, qmv), (om, omv), (nm, nmv)))]
    for d in loads:
        d.start()
    stores = []

    def store(src, dst, sem):
        d = pltpu.make_async_copy(src, dst, sem)
        d.start()
        stores.append(d)

    for i, (corr, ut, e_new, w_new) in enumerate(((corr_q, ut_q, qe_new, qw_new), (corr_o, ut_o, oe_new, ow_new))):
        rows = slice(32 * i, 32 * i + 32)
        one, two, three = parts_of(jnp.concatenate([p[rows, 256 * i : 256 * i + 256], p[rows, 512 + 32 * i : 544 + 32 * i]], axis=1))
        stack = jnp.concatenate([one, one, two, one, two, three], axis=0).T.astype(BF16)
        for k in range(3):
            cut = slice(96 * k, 96 * k + 96)
            decoded = lax.dot_general(stack[cut], lstack[i], (((1,), (0,)), ((), ())), preferred_element_type=F32)
            err[i, cut, :] = corr[cut, :] - decoded
            weight[i, cut, :] = ut[cut, :] - STEP * decoded
            span = pl.ds(96 * k, 96)
            store(err.at[i, span, :], e_new.at[span, :], out_sem.at[0, i, k])
            store(weight.at[i, span, :], w_new.at[span, :], out_sem.at[1, i, k])
    for d in loads:
        d.wait()
    mine = dot(own_left[...], p[...], 1, 0)[0:18]
    for i, (moment, m_new) in enumerate(((qmv, qm_new), (omv, om_new))):
        moment[:, 0:256] = DECAY * moment[:, 0:256] + mine[:, 256 * i : 256 * i + 256]
        moment[:, 256:288] = DECAY * moment[:, 256:288] + mine[:, 512 + 32 * i : 544 + 32 * i]
        store(moment, m_new, sm_sem.at[i])
    gainv[...] = (norms[1] - STEP * norms[0])[0:18]
    store(gainv, gains, sm_sem.at[2])
    flat = iota((24, 128), 0) * 128 + iota((24, 128), 1) - 9 * (lax.axis_index("rep") * 4 + lax.axis_index("shard"))
    for k in range(9):
        nmom[k] = DECAY * nmv[k] + jnp.sum(jnp.where(flat == k, norms[0], 0.0))
    for d in stores:
        d.wait()


def per_device(qg, og, qe, oe, qb, ob, qm, om, qw, ow, ng, nm, nw):
    hbm = pl.BlockSpec(memory_space=pltpu.HBM)
    vmem = pl.BlockSpec(memory_space=pltpu.VMEM)
    smem = pl.BlockSpec(memory_space=pltpu.SMEM)
    sem = pltpu.SemaphoreType.DMA

    def buf(*shape):
        return pltpu.VMEM(shape, F32)

    def turned(array):
        return jnp.swapaxes(array, 1, 2)[0]

    out = jax.ShapeDtypeStruct
    passed = pl.pallas_call(
        communicate,
        out_shape=tuple([out((288, 1152), F32)] * 4)
        + (
            out((2, 192, 1152), BF16),
            out((64, 640), F32),
            out((24, 64), F32),
            out((2, 24, 128), F32),
        ),
        in_specs=[hbm] * 13,
        out_specs=tuple([vmem] * 8),
        scratch_shapes=[
            buf(2, 288, 1152),
            buf(32, 288),
            buf(32, 288),
            buf(18, 288),
            buf(18, 288),
            buf(18, 288),
            buf(18, 288),
            buf(1, 1, 2304),
            pltpu.SMEM((9,), F32),
            pltpu.SMEM((9,), F32),
            buf(5, 1152, 128),
            buf(5, 576, 128),
            buf(5, 2, 72, 128),
            buf(5, 2, 72, 128),
            buf(5, 2, 72, 128),
            buf(5, 2, 72, 128),
            buf(5, 152, 128),
            buf(5, 7, 24, 128),
            buf(24, 640),
            buf(64, 640),
            buf(4, 48, 128),
            buf(24, 640),
            buf(4, 24, 640),
            buf(72, 640),
            buf(1152, 640),
            buf(2, 4, 24, 128),
            buf(2, 8, 8, 384),
            buf(2, 8, 8, 384),
            buf(2, 8, 8, 384),
            buf(2, 8, 8, 384),
            buf(2, 32, 768),
            buf(8, 24, 128),
            buf(72, 128),
            buf(8, 72, 128),
            buf(1152, 128),
            sem((2, 6)),
            sem((9,)),
            sem((5,)), sem((5,)),
            sem((5, 6)), sem((5, 6)),
            sem((5, 7)), sem((5, 7)),
            sem((3,)), sem((3,)),
            sem((4,)), sem((4,)),
            sem((2, 4)), sem((2, 4)),
            sem((8,)), sem((8,)),
            sem,
            sem((2, 3)), sem((2, 3)),
            sem((2, 7)), sem((2, 7)),
            sem((2, 7)), sem((2, 7)),
            sem((2, 7)), sem((2, 7)),
            sem((7,)), sem((7,)),
            sem((7,)), sem((7,)),
        ],
        compiler_params=pltpu.CompilerParams(collective_id=0, has_side_effects=True, vmem_limit_bytes=28 << 20),
        name="communicate",
    )(*[pltpu.with_memory_space_constraint(x, pltpu.HBM) for x in (turned(qg), turned(og), turned(qe), turned(oe), qb.T, ob.T, qm, om, qw, ow, ng, nm, nw)])

    qw_new, ow_new, qm_new, om_new, qe_new, oe_new, gains, nmom = pl.pallas_call(
        decode,
        out_shape=(
            out((288, 1152), F32),
            out((288, 1152), F32),
            out((18, 288), F32),
            out((18, 288), F32),
            out((288, 1152), F32),
            out((288, 1152), F32),
            out((18, 128), F32),
            out((9,), F32),
        ),
        in_specs=[vmem] * 8 + [hbm] * 3,
        out_specs=tuple([hbm] * 7) + (smem,),
        scratch_shapes=[
            buf(2, 288, 1152),
            buf(2, 288, 1152),
            buf(18, 288),
            buf(18, 288),
            buf(18, 128),
            pltpu.SMEM((9,), F32),
            sem((3,)),
            sem((2, 2, 3)),
            sem((3,)),
        ],
        compiler_params=pltpu.CompilerParams(vmem_limit_bytes=24 << 20),
        name="decode",
    )(*passed, qm, om, nm)

    def back(array):
        return array.T[None]

    return qw_new.T, ow_new.T, qm_new, om_new, back(qe_new), back(oe_new), gains.reshape(-1), nmom


def solution(mesh):
    return jax.shard_map(
        per_device,
        mesh=mesh,
        in_specs=(
            P("rep", None, "shard"),
            P("rep", None, "shard"),
            P("rep", None, "shard"),
            P("rep", None, "shard"),
            P("shard", None),
            P("shard", None),
            P("rep", "shard"),
            P("rep", "shard"),
            P("rep", "shard"),
            P("rep", "shard"),
            P("rep", "shard", None),
            P(("rep", "shard")),
            P(("rep", "shard")),
        ),
        out_specs=(
            P(None, "shard"),
            P(None, "shard"),
            P("rep", "shard"),
            P("rep", "shard"),
            P("rep", None, "shard"),
            P("rep", None, "shard"),
            P(),
            P(("rep", "shard")),
        ),
        check_vma=False,
    )
```

```python
import functools

import jax
import jax.numpy as jnp
from jax import lax
from jax.experimental import pallas as pl
from jax.experimental.pallas import tpu as pltpu
from jax.sharding import PartitionSpec as P

MESH = pl.DeviceIdType.MESH
F32 = jnp.float32
BF16 = jnp.bfloat16
HI = lax.Precision.HIGHEST
DECAY = 0.9
STEP = 0.1
NZ, NY, NX = 8, 4, 4
STARTS = [2 * z + (z + 7) // 8 + (z + 3) // 8 for z in range(NZ)]
COUNTS = [24 if z % 4 == 0 else 16 for z in range(NZ)]


def dot(a, b, ca, cb):
    return lax.dot_general(a, b, (((ca,), (cb,)), ((), ())), precision=HI, preferred_element_type=F32)


def iota(shape, axis):
    return lax.broadcasted_iota(jnp.int32, shape, axis)


def parts_of(value):
    one = value.astype(BF16).astype(F32)
    two = (value - one).astype(BF16).astype(F32)
    three = (value - one - two).astype(BF16).astype(F32)
    return one, two, three


def rows_of(z):
    return pl.multiple_of(8 * (2 * z + (z + 7) // 8 + (z + 3) // 8), 8)


def inverse_factor(gram):
    lane, row = iota((32, 128), 1), iota((32, 128), 0)
    is_q = (lane // 32) % 2 == 0
    is_q1 = is_q[:1]
    eye = jnp.where((lane >= 64) & (lane % 32 == row), 1.0, 0.0).astype(F32)
    work = jnp.concatenate([gram, eye[:, 64:]], axis=1)
    for k in range(32):
        pivot_row = work[k : k + 1]
        pivot = jnp.where(is_q1, pivot_row[:, k : k + 1], pivot_row[:, 32 + k : 33 + k])
        column = jnp.where(is_q, work[:, k : k + 1], work[:, 32 + k : 33 + k])
        work = work - jnp.where(row > k, column, 0.0) * (pivot_row / pivot)
    dq = jnp.sum(jnp.where(lane == row, work, 0.0), axis=1, keepdims=True)
    do = jnp.sum(jnp.where(lane == row + 32, work, 0.0), axis=1, keepdims=True)
    scale = 1.0 / jnp.sqrt(jnp.where(is_q, dq, do))
    return (work * scale)[:, 64:]


def block_diagonal(pair):
    lane = iota((32, 64), 1)
    return jnp.concatenate([jnp.where(lane < 32, pair, 0.0), jnp.where(lane >= 32, pair, 0.0)], axis=0)


def communicate(
    qg, og, qe, oe, qb, ob, qm, om, qw, ow, ng, nm, nw,
    corr_q, corr_o, ut_q, ut_o, lstack, p_out, own_left, norm_out,
    err, qbv, obv, qmv, omv, qwv, owv, ngv, nmv, nwv, full, rcv, ya, yb, yc, zbuf, zrecv, zmore, tpack, e0,
    nx, upk, uz, uc, uall, lx, gram_g, gram_z, rsend, rrecv, rz, rag, rt, lgz, lfold, lsc, l2,
    in_sem, sm_sem, s_core, r_core, s_y, r_y, s_z, r_z, s_zm, r_zm, s_nx, r_nx, s_uz, r_uz, s_uy, r_uy, s_uc, r_uc,
    s_lx, r_lx, s_gg, r_gg, s_gz, r_gz, s_rg, r_rg, s_rz, r_rz, s_ra, r_ra, s_lz, r_lz, s_lg, r_lg,
):
    r = lax.axis_index("rep")
    s = lax.axis_index("shard")
    z, g = r // 8, r % 8
    y, c = g // 2, g % 2
    partner = r + 1 - 2 * c
    sends = []

    def rep_of(zz, yy, cc):
        return zz * 8 + yy * 2 + cc

    def copy(src, dst, ssem, rsem, rep, shard):
        d = pltpu.make_async_remote_copy(src_ref=src, dst_ref=dst, send_sem=ssem, recv_sem=rsem, device_id=(rep, shard), device_id_type=MESH)
        d.start()
        sends.append(d)
        return d

    def arrived(like, sem):
        pltpu.make_async_copy(like, like, sem).wait()

    def post(src, dst, ssem, rsem, rep, shard):
        pltpu.make_async_remote_copy(
            src_ref=src, dst_ref=dst, send_sem=ssem, recv_sem=rsem, device_id=(rep, shard), device_id_type=MESH
        ).start()

    def over_g(k):
        return z * 8 + (g + k) % 8

    def over_z(k):
        return ((z + k) % NZ) * 8 + g

    def over_x(k):
        return (s + k) % NX

    barrier = pltpu.get_barrier_semaphore()
    for k in (4, 3, 5, 2, 6, 1, 7):
        pl.semaphore_signal(barrier, inc=1, device_id=(over_z(k), s), device_id_type=MESH)
        pl.semaphore_signal(barrier, inc=1, device_id=(over_g(k), s), device_id_type=MESH)
    for k in (2, 1, 3):
        pl.semaphore_signal(barrier, inc=1, device_id=(r, over_x(k)), device_id_type=MESH)

    def load(src, dst, sem):
        d = pltpu.make_async_copy(src, dst, sem)
        d.start()
        return d

    cuts = ((0, pl.ds(0, 128)), (0, pl.ds(128, 128)), (1, pl.ds(0, 128)), (1, pl.ds(128, 128)), (0, pl.ds(256, 32)), (1, pl.ds(256, 32)))
    loads = []
    for i, (p, cut) in enumerate(cuts):
        grad, error, corr = ((qg, qe, corr_q), (og, oe, corr_o))[p]
        loads.append((load(grad.at[cut], corr.at[cut], in_sem.at[0, i]), load(error.at[cut], err.at[p, cut], in_sem.at[1, i])))

    small = [
        load(src, dst, sm_sem.at[i])
        for i, (src, dst) in enumerate(
            ((qb, qbv), (ob, obv), (qm, qmv), (om, omv), (qw, qwv), (ow, owv), (ng, ngv), (nm, nmv), (nw, nwv))
        )
    ]
    def add_in(i):
        for d in loads[i]:
            d.wait()
        p, cut = cuts[i]
        corr = (corr_q, corr_o)[p]
        corr[cut, :] = corr[cut, :] + err[p, cut, :]

    core_copies = []
    for j in range(5):
        if j < 4:
            add_in(j)
        else:
            add_in(4)
            add_in(5)
        for t in range(9):
            lanes = slice(128 * t, 128 * t + 128)
            if j < 4:
                block = (corr_q, corr_o)[j // 2][128 * (j % 2) : 128 * (j % 2) + 128, lanes]
            else:
                block = jnp.concatenate([corr_q[256:288, lanes], corr_o[256:288, lanes], jnp.zeros((64, 128), F32)], axis=0)
            block = block.T
            if j < 4:
                full[j, lanes, :] = block
            else:
                for row in range(128 * t, 128 * t + 128, 8):
                    piece, at = row // 72, row % 72
                    to = (piece // 2) * 72 + at
                    full[4, to : to + 8, 64 * (piece % 2) : 64 * (piece % 2) + 64] = block[row - 128 * t : row - 128 * t + 8, 0:64]
    for d in small:
        d.wait()
    uq = qwv[...] - (STEP * DECAY) * qmv[...]
    uo = owv[...] - (STEP * DECAY) * omv[...]
    upk[...] = jnp.zeros_like(upk)
    upk[0:18, 0:256] = uq[:, 0:256]
    upk[0:18, 256:512] = uo[:, 0:256]
    upk[0:18, 512:576] = jnp.concatenate([uq[:, 256:288], uo[:, 256:288]], axis=1)
    flat = iota((24, 128), 0) * 128 + iota((24, 128), 1) - 9 * (r * 4 + s)
    gains = jnp.zeros((24, 128), F32)
    for k in range(9):
        gains = jnp.where(flat == k, nwv[k] - (STEP * DECAY) * nmv[k], gains)
    nx[s, 16:24, :] = jnp.zeros((8, 128), F32)
    for i in range(18):
        nx[s, i : i + 1, :] = ngv[0, :, 128 * i : 128 * i + 128]
    nx[s, 24:48, :] = gains
    e0[...] = jnp.zeros_like(e0)
    e0[0:32, 0:256] = qbv[:, 0:256]
    e0[0:32, 512:544] = qbv[:, 256:288]
    e0[32:64, 256:512] = obv[:, 0:256]
    e0[32:64, 544:576] = obv[:, 256:288]

    zbuf[4, :, 64:128] = jnp.zeros((144, 64), F32)
    pl.semaphore_wait(barrier, 17)

    def size(j):
        return 576 if j < 4 else 288

    def core_send(j):
        n = size(j)
        first = pl.multiple_of((1 - c) * n, 8)
        core_copies.append(copy(full.at[j, pl.ds(first, n), :], rcv.at[j, pl.ds(0, n), :], s_core.at[j], r_core.at[j], partner, s))

    def z_pass(t):
        if t >= 2:
            arrived(uz.at[pl.ds(0, 2 if t <= 4 else 1)], r_uz.at[t - 2])
        if t <= 4:
            at = (z + NZ - t + 1) % NZ
            post(uz.at[at], uz.at[at], s_uz, r_uz.at[t - 1], over_z(1), s)
        if t <= 3:
            at = (z + t - 1) % NZ
            post(uz.at[at], uz.at[at], s_uz, r_uz.at[t - 1], over_z(7), s)

    uz[z] = upk[...]
    core_send(0)
    core_send(1)
    z_pass(1)
    for k in (2, 1, 3):
        post(nx.at[s], nx.at[s], s_nx, r_nx, r, over_x(k))

    up, down = rep_of(z, (y + 1) % 4, c), rep_of(z, (y + 3) % 4, c)
    y_plus, y_two, y_minus = (y + 1) % 4, (y + 2) % 4, (y + 3) % 4

    def half_of(j, yy, part):
        block, first, count = (144, 72 * part, 72) if j < 4 else (72, 40 * part, 40 - 8 * part)
        return pl.ds(pl.multiple_of(c * 4 * block + yy * block + first, 8), count)

    def rows_in(j, part):
        return pl.ds(0, 72 if j < 4 else 40 - 8 * part)

    def stage_core(j):
        core_copies[j].wait_recv()

        def body(t, carry):
            rows = pl.ds(pl.multiple_of(c * size(j) + t * 72, 8), 72)
            full[j, rows, :] = full[j, rows, :] + rcv[j, pl.ds(pl.multiple_of(t * 72, 8), 72), :]
            return carry

        lax.fori_loop(0, size(j) // 72, body, 0)
        low, high = rows_in(j, 0), rows_in(j, 1)
        post(full.at[j, half_of(j, y_two, 0), :], ya.at[j, 0, low], s_y, r_y.at[0, j], up, s)
        post(full.at[j, half_of(j, y_two, 1), :], ya.at[j, 1, high], s_y, r_y.at[0, j], down, s)
        post(full.at[j, half_of(j, y_plus, 1), :], yb.at[j, 0, high], s_y, r_y.at[1, j], up, s)
        post(full.at[j, half_of(j, y_minus, 0), :], yb.at[j, 1, low], s_y, r_y.at[1, j], down, s)
        if j + 2 < 5:
            core_send(j + 2)

    def stage_relay(j):
        low, high = rows_in(j, 0), rows_in(j, 1)
        arrived(ya.at[j] if j < 4 else ya.at[j, 0], r_y.at[0, j])
        yc[j, 0, low, :] = full[j, half_of(j, y_plus, 0), :] + ya[j, 0, low, :]
        post(yc.at[j, 0, low], yb.at[j, 2, low], s_y, r_y.at[1, j], up, s)
        yc[j, 1, high, :] = full[j, half_of(j, y_minus, 1), :] + ya[j, 1, high, :]
        post(yc.at[j, 1, high], yb.at[j, 3, high], s_y, r_y.at[1, j], down, s)

    def stage_z(j):
        low, high = rows_in(j, 0), rows_in(j, 1)
        arrived(yb.at[j] if j < 4 else yb.at[j, pl.ds(0, 2)], r_y.at[1, j])
        first = full[j, half_of(j, y, 0), :] + yb[j, 2, low, :] + yb[j, 1, low, :]
        second = full[j, half_of(j, y, 1), :] + yb[j, 0, high, :] + yb[j, 3, high, :]
        if j < 4:
            zbuf[j, 0:72, :] = first
            zbuf[j, 72:144, :] = second
        else:
            for at, part in ((0, first), (40, second)):
                n = part.shape[0]
                zbuf[j, at : at + n, 0:64] = part[:, 0:64]
                zbuf[j, 72 + at : 72 + at + n, 0:64] = part[:, 64:128]
        for k in (4, 3, 5, 2, 6, 1, 7):
            begin = rows_of((z + k) % NZ)
            post(zbuf.at[j, pl.ds(begin, 16), :], zrecv.at[j, k - 1], s_z.at[j], r_z.at[j], over_z(k), s)

            @pl.when((z + k) % 4 == 0)
            def _():
                post(zbuf.at[j, pl.ds(pl.multiple_of(begin + 16, 8), 8), :], zmore.at[j, k - 1], s_zm, r_zm.at[j], over_z(k), s)

    def stage_total(j):
        lanes = slice(128 * j, 128 * j + 128)
        arrived(zrecv.at[j], r_z.at[j])
        value = zbuf[j, pl.ds(rows_of(z), 16), :]
        for k in range(7):
            value = value + zrecv[j, k]
        tpack[0:16, lanes] = value

        @pl.when(z % 4 == 0)
        def _():
            arrived(zmore.at[j], r_zm.at[j])
            value = zbuf[j, pl.ds(pl.multiple_of(rows_of(z) + 16, 8), 8), :]
            for k in range(7):
                value = value + zmore[j, k]
            tpack[16:24, lanes] = value

        @pl.when(z % 4 != 0)
        def _():
            tpack[16:24, lanes] = jnp.zeros((8, 128), F32)

    def u_compact():
        z_pass(5)
        for zz in range(NZ):
            uc[g, 18 * zz : 18 * zz + 18, :] = uz[zz, 0:18, :]
        post(uc.at[g], uc.at[g], s_uy, r_uy.at[0], up, s)
        post(uc.at[g], uc.at[g], s_uy, r_uy.at[1], down, s)
        post(uc.at[g], uc.at[g], s_uc, r_uc.at[0], partner, s)

    def u_relay():
        minus, plus = y_minus * 2 + c, y_plus * 2 + c
        low, high = pl.ds(0, 72), pl.ds(72, 72)
        arrived(uc.at[0], r_uy.at[0])
        post(uc.at[minus, low], uc.at[minus, low], s_uy, r_uy.at[2], up, s)
        post(uc.at[minus], uc.at[minus], s_uc, r_uc.at[1], partner, s)
        arrived(uc.at[0], r_uy.at[1])
        post(uc.at[plus, high], uc.at[plus, high], s_uy, r_uy.at[2], down, s)
        post(uc.at[plus], uc.at[plus], s_uc, r_uc.at[1], partner, s)

    def u_last():
        arrived(uc.at[0], r_uy.at[2])
        two = y_two * 2 + c
        post(uc.at[two], uc.at[two], s_uc, r_uc.at[2], partner, s)

    def u_turn():
        arrived(uc.at[0], r_uc.at[0])
        arrived(uc.at[pl.ds(0, 2)], r_uc.at[1])
        arrived(uc.at[0], r_uc.at[2])
        for zz in range(NZ):
            for gg in range(8):
                to = 144 * zz + 18 * gg
                uall[to : to + 18, :] = uc[gg, 18 * zz : 18 * zz + 18, :]
        for t in range(9):
            rows = slice(128 * t, 128 * t + 128)
            for j in range(4):
                (ut_q, ut_o)[j // 2][128 * (j % 2) : 128 * (j % 2) + 128, rows] = uall[rows, 128 * j : 128 * j + 128].T
            tails = uall[rows, 512:640].T
            ut_q[256:288, rows] = tails[0:32]
            ut_o[256:288, rows] = tails[32:64]

    stage_core(0)
    stage_core(1)
    stage_relay(0)
    stage_core(2)
    z_pass(2)
    stage_relay(1)
    stage_z(0)
    stage_core(3)
    z_pass(3)
    stage_relay(2)
    stage_z(1)
    stage_core(4)
    stage_relay(3)
    stage_z(2)
    z_pass(4)
    stage_relay(4)
    stage_z(3)
    stage_z(4)
    u_compact()
    for j in range(5):
        stage_total(j)

    lane = iota((32, 640), 1)
    of_q = (lane < 256) | ((lane >= 512) & (lane < 544))
    of_o = ((lane >= 256) & (lane < 512)) | ((lane >= 544) & (lane < 576))

    def across(i, partial):
        lx[i, s, :, 0:64] = partial
        for k in (2, 1, 3):
            post(lx.at[i, s], lx.at[i, s], s_lx.at[i], r_lx.at[i], r, over_x(k))

    def left_of(i):
        arrived(lx.at[i, pl.ds(0, 3)], r_lx.at[i])
        return ((lx[i, 0] + lx[i, 1]) + (lx[i, 2] + lx[i, 3]))[:, 0:64]

    def to_g(src, dst, ssem, rsem):
        for k in (4, 5, 3, 2, 6, 7, 1):
            post(src(k), dst, ssem, rsem, over_g(k), s)

    def to_z(src, dst, ssem, rsem):
        for k in (4, 3, 5, 2, 6, 1, 7):
            post(src, dst, ssem, rsem, over_z(k), s)

    def sum_of(v):
        return ((v[0] + v[1]) + (v[2] + v[3])) + ((v[4] + v[5]) + (v[6] + v[7]))

    def total_of(slots, i):
        return sum_of([slots[i, k] for k in range(8)])

    def right_begin(i, left, extra):
        tpack[:, 576:640] = left
        both = dot(left.T, tpack[...], 1, 0)
        right = jnp.where(of_q, both[0:32], both[32:64])
        gram = jnp.where(lane[0:32, 0:64] < 32, both[0:32, 576:640], both[32:64, 576:640])
        if i == 0:
            right = jnp.concatenate([right[:, 0:576], gram], axis=1)
        else:
            gram_g[g, :, 0:64] = gram[0:16]
            gram_g[g, :, 64:128] = gram[16:32]
        for yy in range(4):
            rsend[i, 2 * yy] = right[8 * yy : 8 * yy + 8, 0:384]
            rsend[i, 2 * yy + 1, :, 0:256] = right[8 * yy : 8 * yy + 8, 384:640]
            rsend[i, 2 * yy + 1, :, 256:384] = extra[8 * yy : 8 * yy + 8] if yy < 3 else jnp.zeros((8, 128), F32)
        to_g(lambda k: rsend.at[i, (g + k) % 8], rrecv.at[i, g], s_rg.at[i], r_rg.at[i])
        if i == 1:
            to_g(lambda k: gram_g.at[g], gram_g.at[g], s_gg, r_gg)
        rrecv[i, g] = rsend[i, g]

    def right_middle(i):
        arrived(rrecv.at[i, pl.ds(0, 7)], r_rg.at[i])
        rz[i, z] = total_of(rrecv, i)
        to_z(rz.at[i, z], rz.at[i, z], s_rz.at[i], r_rz.at[i])
        if i == 1:
            arrived(gram_g.at[pl.ds(0, 7)], r_gg)
            gram_z[z] = sum_of([gram_g[k] for k in range(8)])
            to_z(gram_z.at[z], gram_z.at[z], s_gz, r_gz)

    def right_end(i):
        arrived(rz.at[i, pl.ds(0, 7)], r_rz.at[i])
        rag[i, g] = total_of(rz, i)
        to_g(lambda k: rag.at[i, g], rag.at[i, g], s_ra.at[i], r_ra.at[i])

    def gram_read():
        arrived(gram_z.at[pl.ds(0, 7)], r_gz)
        total = sum_of([gram_z[k] for k in range(8)])
        return jnp.concatenate([total[:, 0:64], total[:, 64:128]], axis=0)

    def right_read(i):
        arrived(rag.at[i, pl.ds(0, 7)], r_ra.at[i])
        for yy in range(4):
            for cc in range(2):
                rt[i, 8 * yy : 8 * yy + 8, 384 * cc : 384 * cc + 384] = rag[i, 2 * yy + cc]
        return rt[i, :, 0:640]

    def spread(right):
        return jnp.concatenate([jnp.where(of_q, right, 0.0), jnp.where(of_o, right, 0.0)], axis=0)

    across(0, dot(tpack[...], e0[...], 1, 1))
    arrived(nx.at[pl.ds(0, 3)], r_nx)
    norms = (nx[0] + nx[1]) + (nx[2] + nx[3])
    left = left_of(0)
    right_begin(0, left, norms[0:24])
    right_middle(0)
    u_relay()
    right_end(0)
    right = right_read(0)
    across(1, dot(tpack[...], spread(right), 1, 1))
    u_last()
    factor = block_diagonal(inverse_factor(right[:, 576:640]))
    left = dot(left_of(1), factor, 1, 1)
    right_begin(1, left, norms[24:48])
    lgz[z, :, 0:64] = left
    to_z(lgz.at[z], lgz.at[z], s_lz, r_lz)
    right_middle(1)
    u_turn()
    arrived(lgz.at[pl.ds(0, 7)], r_lz)
    for zz in range(NZ):
        first, count = 8 * STARTS[zz], COUNTS[zz]
        for t in range(count // 8):
            row = first + 8 * t
            value = lgz[zz, 8 * t : 8 * t + 8, 0:64]
            if row < 72:
                lfold[row : row + 8, 0:64] = value
            else:
                lfold[row - 72 : row - 64, 64:128] = value
    h = c * 4 + y
    lsc[h] = lfold[...]
    right_end(1)
    to_g(lambda k: lfold, lsc.at[h], s_lg, r_lg)
    factor = block_diagonal(inverse_factor(gram_read()))
    weighing = dot(factor, factor, 0, 0)
    arrived(lsc.at[pl.ds(0, 7)], r_lg)
    for hh in range(8):
        l2[144 * hh : 144 * hh + 72, 0:64] = lsc[hh, :, 0:64]
        l2[144 * hh + 72 : 144 * hh + 144, 0:64] = lsc[hh, :, 64:128]
    for t in range(9):
        block = l2[128 * t : 128 * t + 128, :].T[0:64]
        one, two, three = parts_of(block)
        for p in range(2):
            rows = slice(32 * p, 32 * p + 32)
            lstack[p, :, 128 * t : 128 * t + 128] = jnp.concatenate(
                [one[rows], two[rows], one[rows], three[rows], two[rows], one[rows]], axis=0
            ).astype(BF16)
    own_first = pl.multiple_of(18 * r // 8 * 8, 8)
    for k in (0, 2, 4, 6):

        @pl.when(18 * r % 8 == k)
        def _():
            own_left[0:18, :] = l2[pl.ds(own_first, 24), 0:64][k : k + 18]

    right = right_read(1)
    p_out[...] = dot(weighing, spread(right), 1, 0)
    norm_out[0] = rt[0, 0:24, 640:768]
    norm_out[1] = rt[1, 0:24, 640:768]
    for d in sends:
        d.wait_send()
    arrived(nx.at[pl.ds(0, 3)], s_nx)
    for j in range(5):
        arrived(zrecv.at[j], s_z.at[j])

    @pl.when(z % 4 == 0)
    def _():
        arrived(zmore.at[pl.ds(0, 5), 0], s_zm)

    @pl.when(z % 4 != 0)
    def _():
        arrived(zmore.at[pl.ds(0, 5), pl.ds(0, 2)], s_zm)

    for i in range(2):
        arrived(lx.at[i, pl.ds(0, 3)], s_lx.at[i])
        arrived(rrecv.at[i, pl.ds(0, 7)], s_rg.at[i])
        arrived(rz.at[i, pl.ds(0, 7)], s_rz.at[i])
        arrived(rag.at[i, pl.ds(0, 7)], s_ra.at[i])
    arrived(lgz.at[pl.ds(0, 7)], s_lz)
    arrived(lsc.at[pl.ds(0, 7)], s_lg)
    arrived(gram_g.at[pl.ds(0, 7)], s_gg)
    arrived(gram_z.at[pl.ds(0, 7)], s_gz)
    arrived(full.at[pl.ds(0, 3), pl.ds(0, 648), :], s_y)
    arrived(uz.at[pl.ds(0, 7)], s_uz)
    arrived(uc.at[pl.ds(0, 3)], s_uy)
    arrived(uc.at[pl.ds(0, 4)], s_uc)


def decode(
    corr_q, corr_o, ut_q, ut_o, lstack, p, own_left, norms, qm, om, nm,
    qw_new, ow_new, qm_new, om_new, qe_new, oe_new, gains, nmom,
    err, weight, qmv, omv, gainv, nmv, in_sem, out_sem, sm_sem,
):
    loads = [pltpu.make_async_copy(src, dst, in_sem.at[i]) for i, (src, dst) in enumerate(((qm, qmv), (om, omv), (nm, nmv)))]
    for d in loads:
        d.start()
    stores = []

    def store(src, dst, sem):
        d = pltpu.make_async_copy(src, dst, sem)
        d.start()
        stores.append(d)

    for i, (corr, ut, e_new, w_new) in enumerate(((corr_q, ut_q, qe_new, qw_new), (corr_o, ut_o, oe_new, ow_new))):
        rows = slice(32 * i, 32 * i + 32)
        one, two, three = parts_of(jnp.concatenate([p[rows, 256 * i : 256 * i + 256], p[rows, 512 + 32 * i : 544 + 32 * i]], axis=1))
        stack = jnp.concatenate([one, one, two, one, two, three], axis=0).T.astype(BF16)
        for k in range(3):
            cut = slice(96 * k, 96 * k + 96)
            decoded = lax.dot_general(stack[cut], lstack[i], (((1,), (0,)), ((), ())), preferred_element_type=F32)
            err[i, cut, :] = corr[cut, :] - decoded
            weight[i, cut, :] = ut[cut, :] - STEP * decoded
            span = pl.ds(96 * k, 96)
            store(err.at[i, span, :], e_new.at[span, :], out_sem.at[0, i, k])
            store(weight.at[i, span, :], w_new.at[span, :], out_sem.at[1, i, k])
    for d in loads:
        d.wait()
    mine = dot(own_left[...], p[...], 1, 0)[0:18]
    for i, (moment, m_new) in enumerate(((qmv, qm_new), (omv, om_new))):
        moment[:, 0:256] = DECAY * moment[:, 0:256] + mine[:, 256 * i : 256 * i + 256]
        moment[:, 256:288] = DECAY * moment[:, 256:288] + mine[:, 512 + 32 * i : 544 + 32 * i]
        store(moment, m_new, sm_sem.at[i])
    gainv[...] = (norms[1] - STEP * norms[0])[0:18]
    store(gainv, gains, sm_sem.at[2])
    flat = iota((24, 128), 0) * 128 + iota((24, 128), 1) - 9 * (lax.axis_index("rep") * 4 + lax.axis_index("shard"))
    for k in range(9):
        nmom[k] = DECAY * nmv[k] + jnp.sum(jnp.where(flat == k, norms[0], 0.0))
    for d in stores:
        d.wait()


def per_device(qg, og, qe, oe, qb, ob, qm, om, qw, ow, ng, nm, nw):
    hbm = pl.BlockSpec(memory_space=pltpu.HBM)
    vmem = pl.BlockSpec(memory_space=pltpu.VMEM)
    smem = pl.BlockSpec(memory_space=pltpu.SMEM)
    sem = pltpu.SemaphoreType.DMA

    def buf(*shape):
        return pltpu.VMEM(shape, F32)

    def turned(array):
        return jnp.swapaxes(array, 1, 2)[0]

    out = jax.ShapeDtypeStruct
    passed = pl.pallas_call(
        communicate,
        out_shape=tuple([out((288, 1152), F32)] * 4)
        + (
            out((2, 192, 1152), BF16),
            out((64, 640), F32),
            out((24, 64), F32),
            out((2, 24, 128), F32),
        ),
        in_specs=[hbm] * 13,
        out_specs=tuple([vmem] * 8),
        scratch_shapes=[
            buf(2, 288, 1152),
            buf(32, 288),
            buf(32, 288),
            buf(18, 288),
            buf(18, 288),
            buf(18, 288),
            buf(18, 288),
            buf(1, 1, 2304),
            pltpu.SMEM((9,), F32),
            pltpu.SMEM((9,), F32),
            buf(5, 1152, 128),
            buf(5, 576, 128),
            buf(5, 2, 72, 128),
            buf(5, 4, 72, 128),
            buf(5, 2, 72, 128),
            buf(5, 144, 128),
            buf(5, 7, 16, 128),
            buf(5, 7, 8, 128),
            buf(24, 640),
            buf(64, 640),
            buf(4, 48, 128),
            buf(24, 640),
            buf(8, 24, 640),
            buf(8, 144, 640),
            buf(1152, 640),
            buf(2, 4, 24, 128),
            buf(8, 16, 128),
            buf(8, 16, 128),
            buf(2, 8, 8, 384),
            buf(2, 8, 8, 384),
            buf(2, 8, 8, 384),
            buf(2, 8, 8, 384),
            buf(2, 32, 768),
            buf(8, 24, 128),
            buf(72, 128),
            buf(8, 72, 128),
            buf(1152, 128),
            sem((2, 6)),
            sem((9,)),
            sem((5,)), sem((5,)),
            sem, sem((2, 5)),
            sem((5,)), sem((5,)),
            sem, sem((5,)),
            sem, sem,
            sem, sem((4,)),
            sem, sem((3,)),
            sem, sem((3,)),
            sem((2,)), sem((2,)),
            sem, sem,
            sem, sem,
            sem((2,)), sem((2,)),
            sem((2,)), sem((2,)),
            sem((2,)), sem((2,)),
            sem, sem,
            sem, sem,
        ],
        compiler_params=pltpu.CompilerParams(collective_id=0, has_side_effects=True, vmem_limit_bytes=28 << 20),
        name="communicate",
    )(*[pltpu.with_memory_space_constraint(x, pltpu.HBM) for x in (turned(qg), turned(og), turned(qe), turned(oe), qb.T, ob.T, qm, om, qw, ow, ng, nm, nw)])

    qw_new, ow_new, qm_new, om_new, qe_new, oe_new, gains, nmom = pl.pallas_call(
        decode,
        out_shape=(
            out((288, 1152), F32),
            out((288, 1152), F32),
            out((18, 288), F32),
            out((18, 288), F32),
            out((288, 1152), F32),
            out((288, 1152), F32),
            out((18, 128), F32),
            out((9,), F32),
        ),
        in_specs=[vmem] * 8 + [hbm] * 3,
        out_specs=tuple([hbm] * 7) + (smem,),
        scratch_shapes=[
            buf(2, 288, 1152),
            buf(2, 288, 1152),
            buf(18, 288),
            buf(18, 288),
            buf(18, 128),
            pltpu.SMEM((9,), F32),
            sem((3,)),
            sem((2, 2, 3)),
            sem((3,)),
        ],
        compiler_params=pltpu.CompilerParams(vmem_limit_bytes=24 << 20),
        name="decode",
    )(*passed, qm, om, nm)

    def back(array):
        return array.T[None]

    return qw_new.T, ow_new.T, qm_new, om_new, back(qe_new), back(oe_new), gains.reshape(-1), nmom


def solution(mesh):
    return jax.shard_map(
        per_device,
        mesh=mesh,
        in_specs=(
            P("rep", None, "shard"),
            P("rep", None, "shard"),
            P("rep", None, "shard"),
            P("rep", None, "shard"),
            P("shard", None),
            P("shard", None),
            P("rep", "shard"),
            P("rep", "shard"),
            P("rep", "shard"),
            P("rep", "shard"),
            P("rep", "shard", None),
            P(("rep", "shard")),
            P(("rep", "shard")),
        ),
        out_specs=(
            P(None, "shard"),
            P(None, "shard"),
            P("rep", "shard"),
            P("rep", "shard"),
            P("rep", None, "shard"),
            P("rep", None, "shard"),
            P(),
            P(("rep", "shard")),
        ),
        check_vma=False,
    )
```

```python
import functools

import jax
import jax.numpy as jnp
from jax import lax
from jax.experimental import pallas as pl
from jax.experimental.pallas import tpu as pltpu
from jax.sharding import PartitionSpec as P

MESH = pl.DeviceIdType.MESH
F32 = jnp.float32
BF16 = jnp.bfloat16
HI = lax.Precision.HIGHEST
DECAY = 0.9
STEP = 0.1
NZ, NY, NX = 8, 4, 4
STARTS = [2 * z + (z + 7) // 8 + (z + 3) // 8 for z in range(NZ)]
COUNTS = [24 if z % 4 == 0 else 16 for z in range(NZ)]


def dot(a, b, ca, cb):
    return lax.dot_general(a, b, (((ca,), (cb,)), ((), ())), precision=HI, preferred_element_type=F32)


def iota(shape, axis):
    return lax.broadcasted_iota(jnp.int32, shape, axis)


def parts_of(value):
    one = value.astype(BF16).astype(F32)
    two = (value - one).astype(BF16).astype(F32)
    three = (value - one - two).astype(BF16).astype(F32)
    return one, two, three


def rows_of(z):
    return pl.multiple_of(8 * (2 * z + (z + 7) // 8 + (z + 3) // 8), 8)


def inverse_factor(gram):
    lane, row = iota((32, 128), 1), iota((32, 128), 0)
    is_q = (lane // 32) % 2 == 0
    is_q1 = is_q[:1]
    eye = jnp.where((lane >= 64) & (lane % 32 == row), 1.0, 0.0).astype(F32)
    work = jnp.concatenate([gram, eye[:, 64:]], axis=1)
    for k in range(32):
        pivot_row = work[k : k + 1]
        pivot = jnp.where(is_q1, pivot_row[:, k : k + 1], pivot_row[:, 32 + k : 33 + k])
        column = jnp.where(is_q, work[:, k : k + 1], work[:, 32 + k : 33 + k])
        work = work - jnp.where(row > k, column, 0.0) * (pivot_row / pivot)
    dq = jnp.sum(jnp.where(lane == row, work, 0.0), axis=1, keepdims=True)
    do = jnp.sum(jnp.where(lane == row + 32, work, 0.0), axis=1, keepdims=True)
    scale = 1.0 / jnp.sqrt(jnp.where(is_q, dq, do))
    return (work * scale)[:, 64:]


def block_diagonal(pair):
    lane = iota((32, 64), 1)
    return jnp.concatenate([jnp.where(lane < 32, pair, 0.0), jnp.where(lane >= 32, pair, 0.0)], axis=0)


def communicate(
    qg, og, qe, oe, qb, ob, qm, om, qw, ow, ng, nm, nw,
    corr_q, corr_o, ut_q, ut_o, lstack, p_out, own_left, norm_out,
    err, qbv, obv, qmv, omv, qwv, owv, ngv, nmv, nwv, full, rcv, ya, yb, yc, zbuf, zrecv, zmore, tpack, tstack, e0,
    nx, nsend, nrecv, nz, nall, upk, uz, uc, uall, lx, gram_g, gram_z, rsend, rrecv, rz, rag, rt, lgz, lfold, lsc, l2,
    in_sem, sm_sem, s_core, r_core, s_y, r_y, s_z, r_z, s_zm, r_zm, s_nx, r_nx, s_ng, r_ng, s_nz, r_nz, s_na, r_na, s_uz, r_uz, s_uy, r_uy, s_uc, r_uc,
    s_lx, r_lx, s_gg, r_gg, s_gz, r_gz, s_rg, r_rg, s_rz, r_rz, s_ra, r_ra, s_lz, r_lz, s_lg, r_lg,
):
    r = lax.axis_index("rep")
    s = lax.axis_index("shard")
    z, g = r // 8, r % 8
    y, c = g // 2, g % 2
    partner = r + 1 - 2 * c
    sends = []

    def rep_of(zz, yy, cc):
        return zz * 8 + yy * 2 + cc

    def copy(src, dst, ssem, rsem, rep, shard):
        d = pltpu.make_async_remote_copy(src_ref=src, dst_ref=dst, send_sem=ssem, recv_sem=rsem, device_id=(rep, shard), device_id_type=MESH)
        d.start()
        sends.append(d)
        return d

    def arrived(like, sem):
        pltpu.make_async_copy(like, like, sem).wait()

    def post(src, dst, ssem, rsem, rep, shard):
        pltpu.make_async_remote_copy(
            src_ref=src, dst_ref=dst, send_sem=ssem, recv_sem=rsem, device_id=(rep, shard), device_id_type=MESH
        ).start()

    def over_g(k):
        return z * 8 + (g + k) % 8

    def over_z(k):
        return ((z + k) % NZ) * 8 + g

    def over_x(k):
        return (s + k) % NX

    barrier = pltpu.get_barrier_semaphore()
    for k in (4, 3, 5, 2, 6, 1, 7):
        pl.semaphore_signal(barrier, inc=1, device_id=(over_z(k), s), device_id_type=MESH)
        pl.semaphore_signal(barrier, inc=1, device_id=(over_g(k), s), device_id_type=MESH)
    for k in (2, 1, 3):
        pl.semaphore_signal(barrier, inc=1, device_id=(r, over_x(k)), device_id_type=MESH)

    def load(src, dst, sem):
        d = pltpu.make_async_copy(src, dst, sem)
        d.start()
        return d

    cuts = ((0, pl.ds(0, 128)), (0, pl.ds(128, 128)), (1, pl.ds(0, 128)), (1, pl.ds(128, 128)), (0, pl.ds(256, 32)), (1, pl.ds(256, 32)))
    loads = []
    for i, (p, cut) in enumerate(cuts):
        grad, error, corr = ((qg, qe, corr_q), (og, oe, corr_o))[p]
        loads.append((load(grad.at[cut], corr.at[cut], in_sem.at[0, i]), load(error.at[cut], err.at[p, cut], in_sem.at[1, i])))

    small = [
        load(src, dst, sm_sem.at[i])
        for i, (src, dst) in enumerate(
            ((qb, qbv), (ob, obv), (qm, qmv), (om, omv), (qw, qwv), (ow, owv), (ng, ngv), (nm, nmv), (nw, nwv))
        )
    ]
    def add_in(i):
        for d in loads[i]:
            d.wait()
        p, cut = cuts[i]
        corr = (corr_q, corr_o)[p]
        corr[cut, :] = corr[cut, :] + err[p, cut, :]

    core_copies = []

    def pack(j):
        if j < 4:
            add_in(j)
        else:
            add_in(4)
            add_in(5)
        for t in range(9):
            lanes = slice(128 * t, 128 * t + 128)
            if j < 4:
                block = (corr_q, corr_o)[j // 2][128 * (j % 2) : 128 * (j % 2) + 128, lanes]
            else:
                block = jnp.concatenate([corr_q[256:288, lanes], corr_o[256:288, lanes], jnp.zeros((64, 128), F32)], axis=0)
            block = block.T
            if j < 4:
                full[j, lanes, :] = block
            else:
                for row in range(128 * t, 128 * t + 128, 8):
                    piece, at = row // 72, row % 72
                    to = (piece // 2) * 72 + at
                    full[4, to : to + 8, 64 * (piece % 2) : 64 * (piece % 2) + 64] = block[row - 128 * t : row - 128 * t + 8, 0:64]


    def size(j):
        return 576 if j < 4 else 288

    def core_send(j):
        n = size(j)
        first = pl.multiple_of((1 - c) * n, 8)
        core_copies.append(copy(full.at[j, pl.ds(first, n), :], rcv.at[j, pl.ds(0, n), :], s_core.at[j], r_core.at[j], partner, s))

    def z_pass(t):
        if t >= 2:
            arrived(uz.at[pl.ds(0, 2 if t <= 4 else 1)], r_uz.at[t - 2])
        if t <= 4:
            at = (z + NZ - t + 1) % NZ
            post(uz.at[at], uz.at[at], s_uz, r_uz.at[t - 1], over_z(1), s)
        if t <= 3:
            at = (z + t - 1) % NZ
            post(uz.at[at], uz.at[at], s_uz, r_uz.at[t - 1], over_z(7), s)


    def to_g(src, dst, ssem, rsem):
        for k in (4, 5, 3, 2, 6, 7, 1):
            post(src(k), dst, ssem, rsem, over_g(k), s)

    def to_z(src, dst, ssem, rsem):
        for k in (4, 3, 5, 2, 6, 1, 7):
            post(src, dst, ssem, rsem, over_z(k), s)

    def sum_of(v):
        return ((v[0] + v[1]) + (v[2] + v[3])) + ((v[4] + v[5]) + (v[6] + v[7]))

    def norm_g():
        arrived(nx.at[pl.ds(0, 3)], r_nx)
        partial = (nx[0] + nx[1]) + (nx[2] + nx[3])
        for k in range(8):
            nsend[k] = partial[8 * k : 8 * k + 8]
        nrecv[g] = nsend[g]
        to_g(lambda k: nsend.at[(g + k) % 8], nrecv.at[g], s_ng, r_ng)

    def norm_z():
        arrived(nrecv.at[pl.ds(0, 7)], r_ng)
        nz[z] = sum_of([nrecv[k] for k in range(8)])
        to_z(nz.at[z], nz.at[z], s_nz, r_nz)

    def norm_all():
        arrived(nz.at[pl.ds(0, 7)], r_nz)
        nall[g] = sum_of([nz[k] for k in range(8)])
        to_g(lambda k: nall.at[g], nall.at[g], s_na, r_na)

    def norm_read():
        arrived(nall.at[pl.ds(0, 7)], r_na)
        for k in range(3):
            norm_out[0, 8 * k : 8 * k + 8, :] = nall[k]
            norm_out[1, 8 * k : 8 * k + 8, :] = nall[k + 3]

    up, down = rep_of(z, (y + 1) % 4, c), rep_of(z, (y + 3) % 4, c)
    y_plus, y_two, y_minus = (y + 1) % 4, (y + 2) % 4, (y + 3) % 4

    def half_of(j, yy, part):
        block, first, count = (144, 72 * part, 72) if j < 4 else (72, 40 * part, 40 - 8 * part)
        return pl.ds(pl.multiple_of(c * 4 * block + yy * block + first, 8), count)

    def rows_in(j, part):
        return pl.ds(0, 72 if j < 4 else 40 - 8 * part)

    def stage_core(j):
        core_copies[j].wait_recv()

        def body(t, carry):
            rows = pl.ds(pl.multiple_of(c * size(j) + t * 72, 8), 72)
            full[j, rows, :] = full[j, rows, :] + rcv[j, pl.ds(pl.multiple_of(t * 72, 8), 72), :]
            return carry

        lax.fori_loop(0, size(j) // 72, body, 0)
        low, high = rows_in(j, 0), rows_in(j, 1)
        post(full.at[j, half_of(j, y_two, 0), :], ya.at[j, 0, low], s_y, r_y.at[0, j], up, s)
        post(full.at[j, half_of(j, y_two, 1), :], ya.at[j, 1, high], s_y, r_y.at[0, j], down, s)
        post(full.at[j, half_of(j, y_plus, 1), :], yb.at[j, 0, high], s_y, r_y.at[1, j], up, s)
        post(full.at[j, half_of(j, y_minus, 0), :], yb.at[j, 1, low], s_y, r_y.at[1, j], down, s)
        if j + 2 < 5:
            core_send(j + 2)

    def stage_relay(j):
        low, high = rows_in(j, 0), rows_in(j, 1)
        arrived(ya.at[j] if j < 4 else ya.at[j, 0], r_y.at[0, j])
        yc[j, 0, low, :] = full[j, half_of(j, y_plus, 0), :] + ya[j, 0, low, :]
        post(yc.at[j, 0, low], yb.at[j, 2, low], s_y, r_y.at[1, j], up, s)
        yc[j, 1, high, :] = full[j, half_of(j, y_minus, 1), :] + ya[j, 1, high, :]
        post(yc.at[j, 1, high], yb.at[j, 3, high], s_y, r_y.at[1, j], down, s)

    def stage_z(j):
        low, high = rows_in(j, 0), rows_in(j, 1)
        arrived(yb.at[j] if j < 4 else yb.at[j, pl.ds(0, 2)], r_y.at[1, j])
        first = full[j, half_of(j, y, 0), :] + yb[j, 2, low, :] + yb[j, 1, low, :]
        second = full[j, half_of(j, y, 1), :] + yb[j, 0, high, :] + yb[j, 3, high, :]
        if j < 4:
            zbuf[j, 0:72, :] = first
            zbuf[j, 72:144, :] = second
        else:
            for at, part in ((0, first), (40, second)):
                n = part.shape[0]
                zbuf[j, at : at + n, 0:64] = part[:, 0:64]
                zbuf[j, 72 + at : 72 + at + n, 0:64] = part[:, 64:128]
        for k in (4, 3, 5, 2, 6, 1, 7):
            begin = rows_of((z + k) % NZ)
            post(zbuf.at[j, pl.ds(begin, 16), :], zrecv.at[j, k - 1], s_z.at[j], r_z.at[j], over_z(k), s)

            @pl.when((z + k) % 4 == 0)
            def _():
                post(zbuf.at[j, pl.ds(pl.multiple_of(begin + 16, 8), 8), :], zmore.at[j, k - 1], s_zm, r_zm.at[j], over_z(k), s)

    def stage_total(j):
        lanes = slice(128 * j, 128 * j + 128)
        arrived(zrecv.at[j], r_z.at[j])
        value = zbuf[j, pl.ds(rows_of(z), 16), :]
        for k in range(7):
            value = value + zrecv[j, k]
        tpack[0:16, lanes] = value

        @pl.when(z % 4 == 0)
        def _():
            arrived(zmore.at[j], r_zm.at[j])
            value = zbuf[j, pl.ds(pl.multiple_of(rows_of(z) + 16, 8), 8), :]
            for k in range(7):
                value = value + zmore[j, k]
            tpack[16:24, lanes] = value

        @pl.when(z % 4 != 0)
        def _():
            tpack[16:24, lanes] = jnp.zeros((8, 128), F32)

    def pieces(block, first, count, ssem, rsem, rep, step=24):
        for at in range(first, first + count, step):
            post(uc.at[block, pl.ds(at, step)], uc.at[block, pl.ds(at, step)], ssem, rsem, rep, s)

    def u_compact():
        z_pass(5)
        for zz in range(NZ):
            uc[g, 18 * zz : 18 * zz + 18, :] = uz[zz, 0:18, :]
        pieces(g, 0, 72, s_uy, r_uy.at[0], up)
        pieces(g, 72, 72, s_uy, r_uy.at[1], down)
        post(uc.at[g], uc.at[g], s_uc, r_uc.at[0], partner, s)

    def u_relay():
        half = uc.at[0, pl.ds(0, 72)]
        arrived(half, r_uy.at[0])
        pieces(y_minus * 2 + c, 0, 72, s_uy, r_uy.at[2], up)
        arrived(half, r_uy.at[1])
        pieces(y_plus * 2 + c, 72, 72, s_uy, r_uy.at[2], down)

    def u_rest():
        pieces(g, 72, 72, s_uy, r_uy.at[3], up)
        pieces(g, 0, 72, s_uy, r_uy.at[3], down)

    def u_last():
        arrived(uc.at[0], r_uy.at[2])
        arrived(uc.at[0], r_uy.at[3])
        for at in (y_minus, y_two, y_plus):
            post(uc.at[at * 2 + c], uc.at[at * 2 + c], s_uc, r_uc.at[1], partner, s)

    def u_turn():
        arrived(uc.at[0], r_uc.at[0])
        arrived(uc.at[pl.ds(0, 3)], r_uc.at[1])
        for zz in range(NZ):
            for gg in range(8):
                to = 144 * zz + 18 * gg
                uall[to : to + 18, :] = uc[gg, 18 * zz : 18 * zz + 18, :]
        for t in range(9):
            rows = slice(128 * t, 128 * t + 128)
            for j in range(4):
                (ut_q, ut_o)[j // 2][128 * (j % 2) : 128 * (j % 2) + 128, rows] = uall[rows, 128 * j : 128 * j + 128].T
            tails = uall[rows, 512:640].T
            ut_q[256:288, rows] = tails[0:32]
            ut_o[256:288, rows] = tails[32:64]

    pack(0)
    pack(1)
    pl.semaphore_wait(barrier, 17)
    core_send(0)
    core_send(1)
    pack(2)
    stage_core(0)
    pack(3)
    stage_core(1)
    pack(4)
    for d in small:
        d.wait()
    uq = qwv[...] - (STEP * DECAY) * qmv[...]
    uo = owv[...] - (STEP * DECAY) * omv[...]
    upk[...] = jnp.zeros_like(upk)
    upk[0:18, 0:256] = uq[:, 0:256]
    upk[0:18, 256:512] = uo[:, 0:256]
    upk[0:18, 512:576] = jnp.concatenate([uq[:, 256:288], uo[:, 256:288]], axis=1)
    flat = iota((24, 128), 0) * 128 + iota((24, 128), 1) - 9 * (r * 4 + s)
    gains = jnp.zeros((24, 128), F32)
    for k in range(9):
        gains = jnp.where(flat == k, nwv[k] - (STEP * DECAY) * nmv[k], gains)
    nx[s, 16:24, :] = jnp.zeros((8, 128), F32)
    for i in range(18):
        nx[s, i : i + 1, :] = ngv[0, :, 128 * i : 128 * i + 128]
    nx[s, 24:48, :] = gains
    nx[s, 48:64, :] = jnp.zeros((16, 128), F32)
    e0[...] = jnp.zeros_like(e0)
    e0[0:32, 0:256] = qbv[:, 0:256]
    e0[0:32, 512:544] = qbv[:, 256:288]
    e0[32:64, 256:512] = obv[:, 0:256]
    e0[32:64, 544:576] = obv[:, 256:288]

    zbuf[4, :, 64:128] = jnp.zeros((144, 64), F32)
    uz[z] = upk[...]
    z_pass(1)
    for k in (2, 1, 3):
        post(nx.at[s], nx.at[s], s_nx, r_nx, r, over_x(k))
    stage_relay(0)
    stage_core(2)
    z_pass(2)
    stage_relay(1)
    stage_z(0)
    stage_core(3)
    z_pass(3)
    stage_relay(2)
    stage_z(1)
    stage_core(4)
    norm_g()
    stage_relay(3)
    stage_z(2)
    z_pass(4)
    stage_relay(4)
    stage_z(3)
    stage_z(4)
    u_compact()
    norm_z()
    for j in range(5):
        stage_total(j)

    lane = iota((32, 640), 1)
    of_q = (lane < 256) | ((lane >= 512) & (lane < 544))
    of_o = ((lane >= 256) & (lane < 512)) | ((lane >= 544) & (lane < 576))

    def fold_into(ref, value):
        ref[:, 0:64] = value[0:16]
        ref[0:8, 64:128] = value[16:24]

    def unfolded(value):
        return jnp.concatenate([value[:, 0:64], value[0:8, 64:128]], axis=0)

    def across(i, partial):
        fold_into(lx.at[i, s], partial)
        for k in (2, 1, 3):
            post(lx.at[i, s], lx.at[i, s], s_lx.at[i], r_lx.at[i], r, over_x(k))

    def left_of(i):
        arrived(lx.at[i, pl.ds(0, 3)], r_lx.at[i])
        return unfolded((lx[i, 0] + lx[i, 1]) + (lx[i, 2] + lx[i, 3]))

    def total_of(slots, i):
        return sum_of([slots[i, k] for k in range(8)])

    def by_core(do):
        for cc, lanes in ((0, pl.ds(0, 384)), (1, pl.ds(0, 256))):

            @pl.when(c == cc)
            def _():
                do(cc, lanes)

    def right_begin(i, left):
        own = parts_of(left)
        tstack[:, 576:640] = jnp.concatenate([own[k] for k in (0, 1, 0, 2, 1, 0)], axis=0).astype(BF16)
        turned = jnp.concatenate([own[k] for k in (0, 0, 1, 0, 1, 2)], axis=0).T.astype(BF16)
        both = lax.dot_general(turned, tstack[...], (((1,), (0,)), ((), ())), preferred_element_type=F32)
        right = jnp.where(of_q, both[0:32], both[32:64])
        gram = jnp.where(lane[0:32, 0:64] < 32, both[0:32, 576:640], both[32:64, 576:640])
        if i == 0:
            right = jnp.concatenate([right[:, 0:576], gram], axis=1)
        else:
            gram_g[g, :, 0:64] = gram[0:16]
            gram_g[g, :, 64:128] = gram[16:32]
        for yy in range(4):
            rsend[i, 2 * yy] = right[8 * yy : 8 * yy + 8, 0:384]
            rsend[i, 2 * yy + 1, :, 0:256] = right[8 * yy : 8 * yy + 8, 384:640]
        for k in (4, 5, 3, 2, 6, 7, 1):
            to = (g + k) % 8

            @pl.when(to % 2 == 0)
            def _():
                post(rsend.at[i, to], rrecv.at[i, g], s_rg.at[i], r_rg.at[i], over_g(k), s)

            @pl.when(to % 2 == 1)
            def _():
                post(rsend.at[i, to, :, pl.ds(0, 256)], rrecv.at[i, g, :, pl.ds(0, 256)], s_rg.at[i], r_rg.at[i], over_g(k), s)

        if i == 1:
            to_g(lambda k: gram_g.at[g], gram_g.at[g], s_gg, r_gg)
        rrecv[i, g] = rsend[i, g]

    def right_middle(i):
        by_core(lambda cc, lanes: arrived(rrecv.at[i, pl.ds(0, 7), :, lanes], r_rg.at[i]))
        rz[i, z] = total_of(rrecv, i)
        by_core(lambda cc, lanes: to_z(rz.at[i, z, :, lanes], rz.at[i, z, :, lanes], s_rz.at[i], r_rz.at[i]))
        if i == 1:
            arrived(gram_g.at[pl.ds(0, 7)], r_gg)
            gram_z[z] = sum_of([gram_g[k] for k in range(8)])
            to_z(gram_z.at[z], gram_z.at[z], s_gz, r_gz)

    def right_end(i):
        by_core(lambda cc, lanes: arrived(rz.at[i, pl.ds(0, 7), :, lanes], r_rz.at[i]))
        rag[i, g] = total_of(rz, i)
        by_core(lambda cc, lanes: to_g(lambda k: rag.at[i, g, :, lanes], rag.at[i, g, :, lanes], s_ra.at[i], r_ra.at[i]))

    def gram_read():
        arrived(gram_z.at[pl.ds(0, 7)], r_gz)
        total = sum_of([gram_z[k] for k in range(8)])
        return jnp.concatenate([total[:, 0:64], total[:, 64:128]], axis=0)

    def right_read(i):
        @pl.when(c == 0)
        def _():
            arrived(full.at[0, pl.ds(0, 136), :], r_ra.at[i])

        @pl.when(c == 1)
        def _():
            arrived(full.at[0, pl.ds(0, 144), :], r_ra.at[i])

        for yy in range(4):
            rt[i, 8 * yy : 8 * yy + 8, 0:384] = rag[i, 2 * yy]
            rt[i, 8 * yy : 8 * yy + 8, 384:640] = rag[i, 2 * yy + 1, :, 0:256]
        return rt[i, :, 0:640]

    def spread(right):
        return jnp.concatenate([jnp.where(of_q, right, 0.0), jnp.where(of_o, right, 0.0)], axis=0)

    parts = parts_of(tpack[...])
    rows_stack = jnp.concatenate(parts, axis=0).astype(BF16)
    tstack[...] = jnp.concatenate([parts[i] for i in (0, 1, 0, 2, 1, 0)], axis=0).astype(BF16)

    def times_total(basis):
        one, two, three = (v.astype(BF16) for v in parts_of(basis))

        def by(rows, v):
            return lax.dot_general(rows, v, (((1,), (1,)), ((), ())), preferred_element_type=F32)

        a, b, d = by(rows_stack, one), by(rows_stack[0:48], two), by(rows_stack[0:24], three)
        return (a[0:24] + (a[24:48] + b[0:24])) + (a[48:72] + b[24:48] + d)

    across(0, times_total(e0[...]))
    left = left_of(0)
    right_begin(0, left)
    right_middle(0)
    u_relay()
    norm_all()
    right_end(0)
    right = right_read(0)
    across(1, times_total(spread(right)))
    u_rest()
    factor = block_diagonal(inverse_factor(right[:, 576:640]))
    left = dot(left_of(1), factor, 1, 1)
    fold_into(lgz.at[z], left)
    to_z(lgz.at[z], lgz.at[z], s_lz, r_lz)
    right_begin(1, left)
    right_middle(1)
    u_last()
    arrived(lgz.at[pl.ds(0, 7)], r_lz)
    for zz in range(NZ):
        first, count = 8 * STARTS[zz], COUNTS[zz]
        for t in range(count // 8):
            row = first + 8 * t
            value = lgz[zz, 8 * t : 8 * t + 8, 0:64] if t < 2 else lgz[zz, 0:8, 64:128]
            if row < 72:
                lfold[row : row + 8, 0:64] = value
            else:
                lfold[row - 72 : row - 64, 64:128] = value
    h = c * 4 + y
    lsc[h] = lfold[...]
    to_g(lambda k: lfold, lsc.at[h], s_lg, r_lg)
    u_turn()
    right_end(1)
    norm_read()
    factor = block_diagonal(inverse_factor(gram_read()))
    weighing = dot(factor, factor, 0, 0)
    arrived(lsc.at[pl.ds(0, 7)], r_lg)
    for hh in range(8):
        l2[144 * hh : 144 * hh + 72, 0:64] = lsc[hh, :, 0:64]
        l2[144 * hh + 72 : 144 * hh + 144, 0:64] = lsc[hh, :, 64:128]
    for t in range(9):
        block = l2[128 * t : 128 * t + 128, :].T[0:64]
        one, two, three = parts_of(block)
        for p in range(2):
            rows = slice(32 * p, 32 * p + 32)
            lstack[p, :, 128 * t : 128 * t + 128] = jnp.concatenate(
                [one[rows], two[rows], one[rows], three[rows], two[rows], one[rows]], axis=0
            ).astype(BF16)
    own_first = pl.multiple_of(18 * r // 8 * 8, 8)
    for k in (0, 2, 4, 6):

        @pl.when(18 * r % 8 == k)
        def _():
            own_left[0:18, :] = l2[pl.ds(own_first, 24), 0:64][k : k + 18]

    right = right_read(1)
    p_out[...] = dot(weighing, spread(right), 1, 0)
    for d in sends:
        d.wait_send()
    arrived(nx.at[pl.ds(0, 3)], s_nx)
    for j in range(5):
        arrived(zrecv.at[j], s_z.at[j])

    @pl.when(z % 4 == 0)
    def _():
        arrived(zmore.at[pl.ds(0, 5), 0], s_zm)

    @pl.when(z % 4 != 0)
    def _():
        arrived(zmore.at[pl.ds(0, 5), pl.ds(0, 2)], s_zm)

    for i in range(2):
        arrived(lx.at[i, pl.ds(0, 3)], s_lx.at[i])
        by_core(lambda cc, lanes: arrived(full.at[0, pl.ds(0, 136 + 8 * cc), :], s_rg.at[i]))
        by_core(lambda cc, lanes: arrived(rz.at[i, pl.ds(0, 7), :, lanes], s_rz.at[i]))
        by_core(lambda cc, lanes: arrived(rag.at[i, pl.ds(0, 7), :, lanes], s_ra.at[i]))
    arrived(lgz.at[pl.ds(0, 7)], s_lz)
    arrived(lsc.at[pl.ds(0, 7)], s_lg)
    arrived(gram_g.at[pl.ds(0, 7)], s_gg)
    arrived(nrecv.at[pl.ds(0, 7)], s_ng)
    arrived(nz.at[pl.ds(0, 7)], s_nz)
    arrived(nall.at[pl.ds(0, 7)], s_na)
    arrived(gram_z.at[pl.ds(0, 7)], s_gz)
    arrived(full.at[pl.ds(0, 3), pl.ds(0, 648), :], s_y)
    arrived(uz.at[pl.ds(0, 7)], s_uz)
    arrived(uc.at[pl.ds(0, 3)], s_uy)
    arrived(uc.at[pl.ds(0, 4)], s_uc)


def decode(
    corr_q, corr_o, ut_q, ut_o, lstack, p, own_left, norms, qm, om, nm,
    qw_new, ow_new, qm_new, om_new, qe_new, oe_new, gains, nmom,
    err, weight, qmv, omv, gainv, nmv, in_sem, out_sem, sm_sem,
):
    loads = [pltpu.make_async_copy(src, dst, in_sem.at[i]) for i, (src, dst) in enumerate(((qm, qmv), (om, omv), (nm, nmv)))]
    for d in loads:
        d.start()
    stores = []

    def store(src, dst, sem):
        d = pltpu.make_async_copy(src, dst, sem)
        d.start()
        stores.append(d)

    for i, (corr, ut, e_new, w_new) in enumerate(((corr_q, ut_q, qe_new, qw_new), (corr_o, ut_o, oe_new, ow_new))):
        rows = slice(32 * i, 32 * i + 32)
        one, two, three = parts_of(jnp.concatenate([p[rows, 256 * i : 256 * i + 256], p[rows, 512 + 32 * i : 544 + 32 * i]], axis=1))
        stack = jnp.concatenate([one, one, two, one, two, three], axis=0).T.astype(BF16)
        for k in range(5):
            width = 256 if k < 4 else 128
            cut = slice(256 * k, 256 * k + width)
            decoded = lax.dot_general(stack, lstack[i, :, cut], (((1,), (0,)), ((), ())), preferred_element_type=F32)
            err[i, :, cut] = corr[:, cut] - decoded
            weight[i, :, cut] = ut[:, cut] - STEP * decoded
            span = pl.ds(256 * k, width)
            store(err.at[i, :, span], e_new.at[:, span], out_sem.at[0, i, k])
            store(weight.at[i, :, span], w_new.at[:, span], out_sem.at[1, i, k])
    for d in loads:
        d.wait()
    mine = dot(own_left[...], p[...], 1, 0)[0:18]
    for i, (moment, m_new) in enumerate(((qmv, qm_new), (omv, om_new))):
        moment[:, 0:256] = DECAY * moment[:, 0:256] + mine[:, 256 * i : 256 * i + 256]
        moment[:, 256:288] = DECAY * moment[:, 256:288] + mine[:, 512 + 32 * i : 544 + 32 * i]
        store(moment, m_new, sm_sem.at[i])
    gainv[...] = (norms[1] - STEP * norms[0])[0:18]
    store(gainv, gains, sm_sem.at[2])
    flat = iota((24, 128), 0) * 128 + iota((24, 128), 1) - 9 * (lax.axis_index("rep") * 4 + lax.axis_index("shard"))
    for k in range(9):
        nmom[k] = DECAY * nmv[k] + jnp.sum(jnp.where(flat == k, norms[0], 0.0))
    for d in stores:
        d.wait()


def per_device(qg, og, qe, oe, qb, ob, qm, om, qw, ow, ng, nm, nw):
    hbm = pl.BlockSpec(memory_space=pltpu.HBM)
    vmem = pl.BlockSpec(memory_space=pltpu.VMEM)
    smem = pl.BlockSpec(memory_space=pltpu.SMEM)
    sem = pltpu.SemaphoreType.DMA

    def buf(*shape):
        return pltpu.VMEM(shape, F32)

    def turned(array):
        return jnp.swapaxes(array, 1, 2)[0]

    out = jax.ShapeDtypeStruct
    passed = pl.pallas_call(
        communicate,
        out_shape=tuple([out((288, 1152), F32)] * 4)
        + (
            out((2, 192, 1152), BF16),
            out((64, 640), F32),
            out((24, 64), F32),
            out((2, 24, 128), F32),
        ),
        in_specs=[hbm] * 13,
        out_specs=tuple([vmem] * 8),
        scratch_shapes=[
            buf(2, 288, 1152),
            buf(32, 288),
            buf(32, 288),
            buf(18, 288),
            buf(18, 288),
            buf(18, 288),
            buf(18, 288),
            buf(1, 1, 2304),
            pltpu.SMEM((9,), F32),
            pltpu.SMEM((9,), F32),
            buf(5, 1152, 128),
            buf(5, 576, 128),
            buf(5, 2, 72, 128),
            buf(5, 4, 72, 128),
            buf(5, 2, 72, 128),
            buf(5, 144, 128),
            buf(5, 7, 16, 128),
            buf(5, 7, 8, 128),
            buf(24, 640),
            pltpu.VMEM((144, 640), BF16),
            buf(64, 640),
            buf(4, 64, 128),
            buf(8, 8, 128),
            buf(8, 8, 128),
            buf(8, 8, 128),
            buf(8, 8, 128),
            buf(24, 640),
            buf(8, 24, 640),
            buf(8, 144, 640),
            buf(1152, 640),
            buf(2, 4, 16, 128),
            buf(8, 16, 128),
            buf(8, 16, 128),
            buf(2, 8, 8, 384),
            buf(2, 8, 8, 384),
            buf(2, 8, 8, 384),
            buf(2, 8, 8, 384),
            buf(2, 32, 640),
            buf(8, 16, 128),
            buf(72, 128),
            buf(8, 72, 128),
            buf(1152, 128),
            sem((2, 6)),
            sem((9,)),
            sem((5,)), sem((5,)),
            sem, sem((2, 5)),
            sem((5,)), sem((5,)),
            sem, sem((5,)),
            sem, sem,
            sem, sem,
            sem, sem,
            sem, sem,
            sem, sem((4,)),
            sem, sem((4,)),
            sem, sem((2,)),
            sem((2,)), sem((2,)),
            sem, sem,
            sem, sem,
            sem((2,)), sem((2,)),
            sem((2,)), sem((2,)),
            sem((2,)), sem((2,)),
            sem, sem,
            sem, sem,
        ],
        compiler_params=pltpu.CompilerParams(collective_id=0, has_side_effects=True, vmem_limit_bytes=28 << 20),
        name="communicate",
    )(*[pltpu.with_memory_space_constraint(x, pltpu.HBM) for x in (turned(qg), turned(og), turned(qe), turned(oe), qb.T, ob.T, qm, om, qw, ow, ng, nm, nw)])

    qw_new, ow_new, qm_new, om_new, qe_new, oe_new, gains, nmom = pl.pallas_call(
        decode,
        out_shape=(
            out((288, 1152), F32),
            out((288, 1152), F32),
            out((18, 288), F32),
            out((18, 288), F32),
            out((288, 1152), F32),
            out((288, 1152), F32),
            out((18, 128), F32),
            out((9,), F32),
        ),
        in_specs=[vmem] * 8 + [hbm] * 3,
        out_specs=tuple([hbm] * 7) + (smem,),
        scratch_shapes=[
            buf(2, 288, 1152),
            buf(2, 288, 1152),
            buf(18, 288),
            buf(18, 288),
            buf(18, 128),
            pltpu.SMEM((9,), F32),
            sem((3,)),
            sem((2, 2, 5)),
            sem((3,)),
        ],
        compiler_params=pltpu.CompilerParams(vmem_limit_bytes=24 << 20),
        name="decode",
    )(*passed, qm, om, nm)

    def back(array):
        return array.T[None]

    return qw_new.T, ow_new.T, qm_new, om_new, back(qe_new), back(oe_new), gains.reshape(-1), nmom


def solution(mesh):
    return jax.shard_map(
        per_device,
        mesh=mesh,
        in_specs=(
            P("rep", None, "shard"),
            P("rep", None, "shard"),
            P("rep", None, "shard"),
            P("rep", None, "shard"),
            P("shard", None),
            P("shard", None),
            P("rep", "shard"),
            P("rep", "shard"),
            P("rep", "shard"),
            P("rep", "shard"),
            P("rep", "shard", None),
            P(("rep", "shard")),
            P(("rep", "shard")),
        ),
        out_specs=(
            P(None, "shard"),
            P(None, "shard"),
            P("rep", "shard"),
            P("rep", "shard"),
            P("rep", None, "shard"),
            P("rep", None, "shard"),
            P(),
            P(("rep", "shard")),
        ),
        check_vma=False,
    )
```

```python
import functools

import jax
import jax.numpy as jnp
from jax import lax
from jax.experimental import pallas as pl
from jax.experimental.pallas import tpu as pltpu
from jax.sharding import PartitionSpec as P

MESH = pl.DeviceIdType.MESH
F32 = jnp.float32
BF16 = jnp.bfloat16
HI = lax.Precision.HIGHEST
DECAY = 0.9
STEP = 0.1
NZ, NY, NX = 8, 4, 4
STARTS = [2 * z + (z + 7) // 8 + (z + 3) // 8 for z in range(NZ)]
COUNTS = [24 if z % 4 == 0 else 16 for z in range(NZ)]


def dot(a, b, ca, cb):
    return lax.dot_general(a, b, (((ca,), (cb,)), ((), ())), precision=HI, preferred_element_type=F32)


def iota(shape, axis):
    return lax.broadcasted_iota(jnp.int32, shape, axis)


def parts_of(value):
    one = value.astype(BF16).astype(F32)
    two = (value - one).astype(BF16).astype(F32)
    three = (value - one - two).astype(BF16).astype(F32)
    return one, two, three


def rows_of(z):
    return pl.multiple_of(8 * (2 * z + (z + 7) // 8 + (z + 3) // 8), 8)


def inverse_factor(gram):
    lane, row = iota((32, 128), 1), iota((32, 128), 0)
    is_q = (lane // 32) % 2 == 0
    is_q1 = is_q[:1]
    eye = jnp.where((lane >= 64) & (lane % 32 == row), 1.0, 0.0).astype(F32)
    work = jnp.concatenate([gram, eye[:, 64:]], axis=1)
    for k in range(32):
        pivot_row = work[k : k + 1]
        pivot = jnp.where(is_q1, pivot_row[:, k : k + 1], pivot_row[:, 32 + k : 33 + k])
        column = jnp.where(is_q, work[:, k : k + 1], work[:, 32 + k : 33 + k])
        work = work - jnp.where(row > k, column, 0.0) * (pivot_row / pivot)
    dq = jnp.sum(jnp.where(lane == row, work, 0.0), axis=1, keepdims=True)
    do = jnp.sum(jnp.where(lane == row + 32, work, 0.0), axis=1, keepdims=True)
    scale = 1.0 / jnp.sqrt(jnp.where(is_q, dq, do))
    return (work * scale)[:, 64:]


def block_diagonal(pair):
    lane = iota((32, 64), 1)
    return jnp.concatenate([jnp.where(lane < 32, pair, 0.0), jnp.where(lane >= 32, pair, 0.0)], axis=0)


def communicate(
    qg, og, qe, oe, qb, ob, qm, om, qw, ow, ng, nm, nw,
    corr_q, corr_o, ut_q, ut_o, lstack, p_out, own_left, norm_out,
    err, qbv, obv, qmv, omv, qwv, owv, ngv, nmv, nwv, full, rcv, ya, yb, yc, zbuf, zrecv, zmore, tpack, tstack, weigh, e0,
    nx, nsend, nrecv, nz, nall, upk, uz, uc, uall, lx, gram_g, gram_z, rsend, rrecv, rz, rag, rt, lgz, lfold, lsc, l2,
    in_sem, sm_sem, s_core, r_core, s_y, r_y, s_z, r_z, s_zm, r_zm, s_nx, r_nx, s_ng, r_ng, s_nz, r_nz, s_na, r_na, s_uz, r_uz, s_uy, r_uy, s_uc, r_uc,
    s_lx, r_lx, s_gg, r_gg, s_gz, r_gz, s_rg, r_rg, s_rz, r_rz, s_ra, r_ra, s_lz, r_lz, s_lg, r_lg,
):
    r = lax.axis_index("rep")
    s = lax.axis_index("shard")
    z, g = r // 8, r % 8
    y, c = g // 2, g % 2
    partner = r + 1 - 2 * c
    sends = []

    apart = pl.when(r >= 0)

    def rep_of(zz, yy, cc):
        return zz * 8 + yy * 2 + cc

    def copy(src, dst, ssem, rsem, rep, shard):
        d = pltpu.make_async_remote_copy(src_ref=src, dst_ref=dst, send_sem=ssem, recv_sem=rsem, device_id=(rep, shard), device_id_type=MESH)
        d.start()
        sends.append(d)
        return d

    def arrived(like, sem):
        pltpu.make_async_copy(like, like, sem).wait()

    def post(src, dst, ssem, rsem, rep, shard):
        pltpu.make_async_remote_copy(
            src_ref=src, dst_ref=dst, send_sem=ssem, recv_sem=rsem, device_id=(rep, shard), device_id_type=MESH
        ).start()

    def over_g(k):
        return z * 8 + (g + k) % 8

    def over_z(k):
        return ((z + k) % NZ) * 8 + g

    def over_x(k):
        return (s + k) % NX

    barrier = pltpu.get_barrier_semaphore()
    for k in (4, 3, 5, 2, 6, 1, 7):
        pl.semaphore_signal(barrier, inc=1, device_id=(over_z(k), s), device_id_type=MESH)
        pl.semaphore_signal(barrier, inc=1, device_id=(over_g(k), s), device_id_type=MESH)
    for k in (2, 1, 3):
        pl.semaphore_signal(barrier, inc=1, device_id=(r, over_x(k)), device_id_type=MESH)

    def load(src, dst, sem):
        d = pltpu.make_async_copy(src, dst, sem)
        d.start()
        return d

    cuts = ((0, pl.ds(0, 128)), (0, pl.ds(128, 128)), (1, pl.ds(0, 128)), (1, pl.ds(128, 128)), (0, pl.ds(256, 32)), (1, pl.ds(256, 32)))
    loads = []
    for i, (p, cut) in enumerate(cuts):
        grad, error, corr = ((qg, qe, corr_q), (og, oe, corr_o))[p]
        loads.append((load(grad.at[cut], corr.at[cut], in_sem.at[0, i]), load(error.at[cut], err.at[p, cut], in_sem.at[1, i])))

    small = [
        load(src, dst, sm_sem.at[i])
        for i, (src, dst) in enumerate(
            ((qb, qbv), (ob, obv), (qm, qmv), (om, omv), (qw, qwv), (ow, owv), (ng, ngv), (nm, nmv), (nw, nwv))
        )
    ]
    def add_in(i):
        for d in loads[i]:
            d.wait()
        p, cut = cuts[i]
        corr = (corr_q, corr_o)[p]
        corr[cut, :] = corr[cut, :] + err[p, cut, :]

    core_copies = []

    def pack(j):
        if j < 4:
            add_in(j)
        else:
            add_in(4)
            add_in(5)
        for t in range(9):
            lanes = slice(128 * t, 128 * t + 128)
            if j < 4:
                block = (corr_q, corr_o)[j // 2][128 * (j % 2) : 128 * (j % 2) + 128, lanes]
            else:
                block = jnp.concatenate([corr_q[256:288, lanes], corr_o[256:288, lanes], jnp.zeros((64, 128), F32)], axis=0)
            block = block.T
            if j < 4:
                full[j, lanes, :] = block
            else:
                for row in range(128 * t, 128 * t + 128, 8):
                    piece, at = row // 72, row % 72
                    to = (piece // 2) * 72 + at
                    full[4, to : to + 8, 64 * (piece % 2) : 64 * (piece % 2) + 64] = block[row - 128 * t : row - 128 * t + 8, 0:64]


    def size(j):
        return 576 if j < 4 else 288

    def core_send(j):
        n = size(j)
        first = pl.multiple_of((1 - c) * n, 8)
        core_copies.append(copy(full.at[j, pl.ds(first, n), :], rcv.at[j, pl.ds(0, n), :], s_core.at[j], r_core.at[j], partner, s))

    def z_pass(t):
        if t >= 2:
            arrived(uz.at[pl.ds(0, 2 if t <= 4 else 1)], r_uz.at[t - 2])
        if t <= 4:
            at = (z + NZ - t + 1) % NZ
            post(uz.at[at], uz.at[at], s_uz, r_uz.at[t - 1], over_z(1), s)
        if t <= 3:
            at = (z + t - 1) % NZ
            post(uz.at[at], uz.at[at], s_uz, r_uz.at[t - 1], over_z(7), s)


    def to_g(src, dst, ssem, rsem):
        for k in (4, 5, 3, 2, 6, 7, 1):
            post(src(k), dst, ssem, rsem, over_g(k), s)

    def to_z(src, dst, ssem, rsem):
        for k in (4, 3, 5, 2, 6, 1, 7):
            post(src, dst, ssem, rsem, over_z(k), s)

    def sum_of(v):
        return ((v[0] + v[1]) + (v[2] + v[3])) + ((v[4] + v[5]) + (v[6] + v[7]))

    def norm_g():
        arrived(nx.at[pl.ds(0, 3)], r_nx)
        partial = (nx[0] + nx[1]) + (nx[2] + nx[3])
        for k in range(8):
            nsend[k] = partial[8 * k : 8 * k + 8]
        nrecv[g] = nsend[g]
        to_g(lambda k: nsend.at[(g + k) % 8], nrecv.at[g], s_ng, r_ng)

    def norm_z():
        arrived(nrecv.at[pl.ds(0, 7)], r_ng)
        nz[z] = sum_of([nrecv[k] for k in range(8)])
        to_z(nz.at[z], nz.at[z], s_nz, r_nz)

    def norm_all():
        arrived(nz.at[pl.ds(0, 7)], r_nz)
        nall[g] = sum_of([nz[k] for k in range(8)])
        to_g(lambda k: nall.at[g], nall.at[g], s_na, r_na)

    def norm_read():
        arrived(nall.at[pl.ds(0, 7)], r_na)
        for k in range(3):
            norm_out[0, 8 * k : 8 * k + 8, :] = nall[k]
            norm_out[1, 8 * k : 8 * k + 8, :] = nall[k + 3]

    up, down = rep_of(z, (y + 1) % 4, c), rep_of(z, (y + 3) % 4, c)
    y_plus, y_two, y_minus = (y + 1) % 4, (y + 2) % 4, (y + 3) % 4

    def half_of(j, yy, part):
        block, first, count = (144, 72 * part, 72) if j < 4 else (72, 40 * part, 40 - 8 * part)
        return pl.ds(pl.multiple_of(c * 4 * block + yy * block + first, 8), count)

    def rows_in(j, part):
        return pl.ds(0, 72 if j < 4 else 40 - 8 * part)

    def stage_core(j):
        core_copies[j].wait_recv()

        def body(t, carry):
            rows = pl.ds(pl.multiple_of(c * size(j) + t * 72, 8), 72)
            full[j, rows, :] = full[j, rows, :] + rcv[j, pl.ds(pl.multiple_of(t * 72, 8), 72), :]
            return carry

        lax.fori_loop(0, size(j) // 72, body, 0)
        low, high = rows_in(j, 0), rows_in(j, 1)
        post(full.at[j, half_of(j, y_two, 0), :], ya.at[j, 0, low], s_y, r_y.at[0, j], up, s)
        post(full.at[j, half_of(j, y_two, 1), :], ya.at[j, 1, high], s_y, r_y.at[0, j], down, s)
        post(full.at[j, half_of(j, y_plus, 1), :], yb.at[j, 0, high], s_y, r_y.at[1, j], up, s)
        post(full.at[j, half_of(j, y_minus, 0), :], yb.at[j, 1, low], s_y, r_y.at[1, j], down, s)
        if j + 2 < 5:
            core_send(j + 2)

    def stage_relay(j):
        low, high = rows_in(j, 0), rows_in(j, 1)
        arrived(ya.at[j] if j < 4 else ya.at[j, 0], r_y.at[0, j])
        yc[j, 0, low, :] = full[j, half_of(j, y_plus, 0), :] + ya[j, 0, low, :]
        post(yc.at[j, 0, low], yb.at[j, 2, low], s_y, r_y.at[1, j], up, s)
        yc[j, 1, high, :] = full[j, half_of(j, y_minus, 1), :] + ya[j, 1, high, :]
        post(yc.at[j, 1, high], yb.at[j, 3, high], s_y, r_y.at[1, j], down, s)

    def stage_z(j):
        low, high = rows_in(j, 0), rows_in(j, 1)
        arrived(yb.at[j] if j < 4 else yb.at[j, pl.ds(0, 2)], r_y.at[1, j])
        first = full[j, half_of(j, y, 0), :] + yb[j, 2, low, :] + yb[j, 1, low, :]
        second = full[j, half_of(j, y, 1), :] + yb[j, 0, high, :] + yb[j, 3, high, :]
        if j < 4:
            zbuf[j, 0:72, :] = first
            zbuf[j, 72:144, :] = second
        else:
            for at, part in ((0, first), (40, second)):
                n = part.shape[0]
                zbuf[j, at : at + n, 0:64] = part[:, 0:64]
                zbuf[j, 72 + at : 72 + at + n, 0:64] = part[:, 64:128]
        for k in (4, 3, 5, 2, 6, 1, 7):
            begin = rows_of((z + k) % NZ)
            post(zbuf.at[j, pl.ds(begin, 16), :], zrecv.at[j, k - 1], s_z.at[j], r_z.at[j], over_z(k), s)

            @pl.when((z + k) % 4 == 0)
            def _():
                post(zbuf.at[j, pl.ds(pl.multiple_of(begin + 16, 8), 8), :], zmore.at[j, k - 1], s_zm, r_zm.at[j], over_z(k), s)

    def stage_total(j):
        lanes = slice(128 * j, 128 * j + 128)
        arrived(zrecv.at[j], r_z.at[j])
        value = zbuf[j, pl.ds(rows_of(z), 16), :]
        for k in range(7):
            value = value + zrecv[j, k]
        tpack[0:16, lanes] = value

        @pl.when(z % 4 == 0)
        def _():
            arrived(zmore.at[j], r_zm.at[j])
            value = zbuf[j, pl.ds(pl.multiple_of(rows_of(z) + 16, 8), 8), :]
            for k in range(7):
                value = value + zmore[j, k]
            tpack[16:24, lanes] = value

        @pl.when(z % 4 != 0)
        def _():
            tpack[16:24, lanes] = jnp.zeros((8, 128), F32)

    def pieces(block, first, count, ssem, rsem, rep, step=24):
        for at in range(first, first + count, step):
            post(uc.at[block, pl.ds(at, step)], uc.at[block, pl.ds(at, step)], ssem, rsem, rep, s)

    def u_compact():
        z_pass(5)

        @apart
        def _():
            for zz in range(NZ):
                uc[g, 18 * zz : 18 * zz + 18, :] = uz[zz, 0:18, :]

        pieces(g, 0, 72, s_uy, r_uy.at[0], up)
        pieces(g, 72, 72, s_uy, r_uy.at[1], down)
        post(uc.at[g], uc.at[g], s_uc, r_uc.at[0], partner, s)

    def u_relay():
        half = uc.at[0, pl.ds(0, 72)]
        arrived(half, r_uy.at[0])
        pieces(y_minus * 2 + c, 0, 72, s_uy, r_uy.at[2], up)
        arrived(half, r_uy.at[1])
        pieces(y_plus * 2 + c, 72, 72, s_uy, r_uy.at[2], down)

    def u_rest():
        pieces(g, 72, 72, s_uy, r_uy.at[3], up)
        pieces(g, 0, 72, s_uy, r_uy.at[3], down)

    def u_last():
        arrived(uc.at[0], r_uy.at[2])
        arrived(uc.at[0], r_uy.at[3])
        for at in (y_minus, y_two, y_plus):
            post(uc.at[at * 2 + c], uc.at[at * 2 + c], s_uc, r_uc.at[1], partner, s)

    def u_turn():
        arrived(uc.at[0], r_uc.at[0])
        arrived(uc.at[pl.ds(0, 3)], r_uc.at[1])
        for zz in range(NZ):
            for gg in range(8):
                to = 144 * zz + 18 * gg
                uall[to : to + 18, :] = uc[gg, 18 * zz : 18 * zz + 18, :]
        for t in range(9):
            rows = slice(128 * t, 128 * t + 128)
            for j in range(4):
                (ut_q, ut_o)[j // 2][128 * (j % 2) : 128 * (j % 2) + 128, rows] = uall[rows, 128 * j : 128 * j + 128].T
            tails = uall[rows, 512:640].T
            ut_q[256:288, rows] = tails[0:32]
            ut_o[256:288, rows] = tails[32:64]

    pack(0)
    pack(1)
    pl.semaphore_wait(barrier, 17)
    core_send(0)
    core_send(1)
    pack(2)
    stage_core(0)
    pack(3)
    stage_core(1)
    pack(4)
    for d in small:
        d.wait()
    uq = qwv[...] - (STEP * DECAY) * qmv[...]
    uo = owv[...] - (STEP * DECAY) * omv[...]
    upk[...] = jnp.zeros_like(upk)
    upk[0:18, 0:256] = uq[:, 0:256]
    upk[0:18, 256:512] = uo[:, 0:256]
    upk[0:18, 512:576] = jnp.concatenate([uq[:, 256:288], uo[:, 256:288]], axis=1)
    flat = iota((24, 128), 0) * 128 + iota((24, 128), 1) - 9 * (r * 4 + s)
    gains = jnp.zeros((24, 128), F32)
    for k in range(9):
        gains = jnp.where(flat == k, nwv[k] - (STEP * DECAY) * nmv[k], gains)
    nx[s, 16:24, :] = jnp.zeros((8, 128), F32)
    for i in range(18):
        nx[s, i : i + 1, :] = ngv[0, :, 128 * i : 128 * i + 128]
    nx[s, 24:48, :] = gains
    nx[s, 48:64, :] = jnp.zeros((16, 128), F32)
    e0[...] = jnp.zeros_like(e0)
    e0[0:32, 0:256] = qbv[:, 0:256]
    e0[0:32, 512:544] = qbv[:, 256:288]
    e0[32:64, 256:512] = obv[:, 0:256]
    e0[32:64, 544:576] = obv[:, 256:288]

    zbuf[4, :, 64:128] = jnp.zeros((144, 64), F32)
    uz[z] = upk[...]
    z_pass(1)
    for k in (2, 1, 3):
        post(nx.at[s], nx.at[s], s_nx, r_nx, r, over_x(k))
    apart(functools.partial(stage_relay, 0))
    stage_core(2)
    z_pass(2)
    apart(functools.partial(stage_relay, 1))
    apart(functools.partial(stage_z, 0))
    stage_core(3)
    z_pass(3)
    apart(functools.partial(stage_relay, 2))
    apart(functools.partial(stage_z, 1))
    stage_core(4)
    apart(functools.partial(stage_relay, 3))
    apart(functools.partial(stage_z, 2))
    z_pass(4)
    apart(functools.partial(stage_relay, 4))
    apart(functools.partial(stage_z, 3))
    apart(functools.partial(stage_z, 4))
    apart(u_compact)
    for j in range(5):
        apart(functools.partial(stage_total, j))

    lane = iota((32, 640), 1)
    of_q = (lane < 256) | ((lane >= 512) & (lane < 544))
    of_o = ((lane >= 256) & (lane < 512)) | ((lane >= 544) & (lane < 576))

    def fold_into(ref, value):
        ref[:, 0:64] = value[0:16]
        ref[0:8, 64:128] = value[16:24]

    def unfolded(value):
        return jnp.concatenate([value[:, 0:64], value[0:8, 64:128]], axis=0)

    def across(i, partial):
        fold_into(lx.at[i, s], partial)
        for k in (2, 1, 3):
            post(lx.at[i, s], lx.at[i, s], s_lx.at[i], r_lx.at[i], r, over_x(k))

    def left_of(i):
        arrived(lx.at[i, pl.ds(0, 3)], r_lx.at[i])
        return unfolded((lx[i, 0] + lx[i, 1]) + (lx[i, 2] + lx[i, 3]))

    def total_of(slots, i):
        return sum_of([slots[i, k] for k in range(8)])

    def by_core(do):
        for cc, lanes in ((0, pl.ds(0, 384)), (1, pl.ds(0, 256))):

            @pl.when(c == cc)
            def _():
                do(cc, lanes)

    def right_begin(i, left):
        own = parts_of(left)
        tstack[:, 576:640] = jnp.concatenate([own[k] for k in (0, 1, 0, 2, 1, 0)], axis=0).astype(BF16)
        turned = jnp.concatenate([own[k] for k in (0, 0, 1, 0, 1, 2)], axis=0).T.astype(BF16)
        both = lax.dot_general(turned, tstack[...], (((1,), (0,)), ((), ())), preferred_element_type=F32)
        right = jnp.where(of_q, both[0:32], both[32:64])
        gram = jnp.where(lane[0:32, 0:64] < 32, both[0:32, 576:640], both[32:64, 576:640])
        if i == 0:
            right = jnp.concatenate([right[:, 0:576], gram], axis=1)
        else:
            gram_g[g, :, 0:64] = gram[0:16]
            gram_g[g, :, 64:128] = gram[16:32]
        for yy in range(4):
            rsend[i, 2 * yy] = right[8 * yy : 8 * yy + 8, 0:384]
            rsend[i, 2 * yy + 1, :, 0:256] = right[8 * yy : 8 * yy + 8, 384:640]
        for k in (4, 5, 3, 2, 6, 7, 1):
            to = (g + k) % 8

            @pl.when(to % 2 == 0)
            def _():
                post(rsend.at[i, to], rrecv.at[i, g], s_rg.at[i], r_rg.at[i], over_g(k), s)

            @pl.when(to % 2 == 1)
            def _():
                post(rsend.at[i, to, :, pl.ds(0, 256)], rrecv.at[i, g, :, pl.ds(0, 256)], s_rg.at[i], r_rg.at[i], over_g(k), s)

        if i == 1:
            to_g(lambda k: gram_g.at[g], gram_g.at[g], s_gg, r_gg)
        rrecv[i, g] = rsend[i, g]

    def right_middle(i):
        by_core(lambda cc, lanes: arrived(rrecv.at[i, pl.ds(0, 7), :, lanes], r_rg.at[i]))
        rz[i, z] = total_of(rrecv, i)
        by_core(lambda cc, lanes: to_z(rz.at[i, z, :, lanes], rz.at[i, z, :, lanes], s_rz.at[i], r_rz.at[i]))
        if i == 1:
            arrived(gram_g.at[pl.ds(0, 7)], r_gg)
            gram_z[z] = sum_of([gram_g[k] for k in range(8)])
            to_z(gram_z.at[z], gram_z.at[z], s_gz, r_gz)

    def right_end(i):
        by_core(lambda cc, lanes: arrived(rz.at[i, pl.ds(0, 7), :, lanes], r_rz.at[i]))
        rag[i, g] = total_of(rz, i)
        by_core(lambda cc, lanes: to_g(lambda k: rag.at[i, g, :, lanes], rag.at[i, g, :, lanes], s_ra.at[i], r_ra.at[i]))

    def gram_read():
        arrived(gram_z.at[pl.ds(0, 7)], r_gz)
        total = sum_of([gram_z[k] for k in range(8)])
        return jnp.concatenate([total[:, 0:64], total[:, 64:128]], axis=0)

    def right_read(i):
        @pl.when(c == 0)
        def _():
            arrived(full.at[0, pl.ds(0, 136), :], r_ra.at[i])

        @pl.when(c == 1)
        def _():
            arrived(full.at[0, pl.ds(0, 144), :], r_ra.at[i])

        for yy in range(4):
            rt[i, 8 * yy : 8 * yy + 8, 0:384] = rag[i, 2 * yy]
            rt[i, 8 * yy : 8 * yy + 8, 384:640] = rag[i, 2 * yy + 1, :, 0:256]
        return rt[i, :, 0:640]

    def spread(right):
        return jnp.concatenate([jnp.where(of_q, right, 0.0), jnp.where(of_o, right, 0.0)], axis=0)

    parts = parts_of(tpack[...])
    rows_stack = jnp.concatenate(parts, axis=0).astype(BF16)
    tstack[...] = jnp.concatenate([parts[i] for i in (0, 1, 0, 2, 1, 0)], axis=0).astype(BF16)

    def times_total(basis):
        one, two, three = (v.astype(BF16) for v in parts_of(basis))

        def by(rows, v):
            return lax.dot_general(rows, v, (((1,), (1,)), ((), ())), preferred_element_type=F32)

        a, b, d = by(rows_stack, one), by(rows_stack[0:48], two), by(rows_stack[0:24], three)
        return (a[0:24] + (a[24:48] + b[0:24])) + (a[48:72] + b[24:48] + d)

    across(0, times_total(e0[...]))
    @apart
    def _():
        right_begin(0, left_of(0))

    apart(lambda: right_middle(0))
    apart(u_relay)
    apart(norm_g)
    apart(lambda: right_end(0))
    apart(norm_z)
    right = right_read(0)
    across(1, times_total(spread(right)))
    u_rest()
    factor = block_diagonal(inverse_factor(right[:, 576:640]))
    left = dot(left_of(1), factor, 1, 1)
    fold_into(lgz.at[z], left)
    to_z(lgz.at[z], lgz.at[z], s_lz, r_lz)
    right_begin(1, left)
    apart(lambda: right_middle(1))
    apart(u_last)
    apart(norm_all)
    arrived(lgz.at[pl.ds(0, 7)], r_lz)
    for zz in range(NZ):
        first, count = 8 * STARTS[zz], COUNTS[zz]
        for t in range(count // 8):
            row = first + 8 * t
            value = lgz[zz, 8 * t : 8 * t + 8, 0:64] if t < 2 else lgz[zz, 0:8, 64:128]
            if row < 72:
                lfold[row : row + 8, 0:64] = value
            else:
                lfold[row - 72 : row - 64, 64:128] = value
    h = c * 4 + y
    lsc[h] = lfold[...]
    to_g(lambda k: lfold, lsc.at[h], s_lg, r_lg)
    apart(u_turn)
    apart(lambda: right_end(1))
    apart(norm_read)

    @apart
    def _():
        factor = block_diagonal(inverse_factor(gram_read()))
        weigh[...] = dot(factor, factor, 0, 0)

    arrived(lsc.at[pl.ds(0, 7)], r_lg)
    @apart
    def _():
        for hh in range(8):
            l2[144 * hh : 144 * hh + 72, 0:64] = lsc[hh, :, 0:64]
            l2[144 * hh + 72 : 144 * hh + 144, 0:64] = lsc[hh, :, 64:128]
        for t in range(9):
            block = l2[128 * t : 128 * t + 128, :].T[0:64]
            one, two, three = parts_of(block)
            for p in range(2):
                rows = slice(32 * p, 32 * p + 32)
                lstack[p, :, 128 * t : 128 * t + 128] = jnp.concatenate(
                    [one[rows], two[rows], one[rows], three[rows], two[rows], one[rows]], axis=0
                ).astype(BF16)

    own_first = pl.multiple_of(18 * r // 8 * 8, 8)
    for k in (0, 2, 4, 6):

        @pl.when(18 * r % 8 == k)
        def _():
            own_left[0:18, :] = l2[pl.ds(own_first, 24), 0:64][k : k + 18]

    right = right_read(1)
    p_out[...] = dot(weigh[...], spread(right), 1, 0)
    for d in sends:
        d.wait_send()
    arrived(nx.at[pl.ds(0, 3)], s_nx)
    for j in range(5):
        arrived(zrecv.at[j], s_z.at[j])

    @pl.when(z % 4 == 0)
    def _():
        arrived(zmore.at[pl.ds(0, 5), 0], s_zm)

    @pl.when(z % 4 != 0)
    def _():
        arrived(zmore.at[pl.ds(0, 5), pl.ds(0, 2)], s_zm)

    for i in range(2):
        arrived(lx.at[i, pl.ds(0, 3)], s_lx.at[i])
        by_core(lambda cc, lanes: arrived(full.at[0, pl.ds(0, 136 + 8 * cc), :], s_rg.at[i]))
        by_core(lambda cc, lanes: arrived(rz.at[i, pl.ds(0, 7), :, lanes], s_rz.at[i]))
        by_core(lambda cc, lanes: arrived(rag.at[i, pl.ds(0, 7), :, lanes], s_ra.at[i]))
    arrived(lgz.at[pl.ds(0, 7)], s_lz)
    arrived(lsc.at[pl.ds(0, 7)], s_lg)
    arrived(gram_g.at[pl.ds(0, 7)], s_gg)
    arrived(nrecv.at[pl.ds(0, 7)], s_ng)
    arrived(nz.at[pl.ds(0, 7)], s_nz)
    arrived(nall.at[pl.ds(0, 7)], s_na)
    arrived(gram_z.at[pl.ds(0, 7)], s_gz)
    arrived(full.at[pl.ds(0, 3), pl.ds(0, 648), :], s_y)
    arrived(uz.at[pl.ds(0, 7)], s_uz)
    arrived(uc.at[pl.ds(0, 3)], s_uy)
    arrived(uc.at[pl.ds(0, 4)], s_uc)


def decode(
    corr_q, corr_o, ut_q, ut_o, lstack, p, own_left, norms, qm, om, nm,
    qw_new, ow_new, qm_new, om_new, qe_new, oe_new, gains, nmom,
    err, weight, qmv, omv, gainv, nmv, in_sem, out_sem, sm_sem,
):
    loads = [pltpu.make_async_copy(src, dst, in_sem.at[i]) for i, (src, dst) in enumerate(((qm, qmv), (om, omv), (nm, nmv)))]
    for d in loads:
        d.start()
    stores = []

    def store(src, dst, sem):
        d = pltpu.make_async_copy(src, dst, sem)
        d.start()
        stores.append(d)

    for i, (corr, ut, e_new, w_new) in enumerate(((corr_q, ut_q, qe_new, qw_new), (corr_o, ut_o, oe_new, ow_new))):
        rows = slice(32 * i, 32 * i + 32)
        one, two, three = parts_of(jnp.concatenate([p[rows, 256 * i : 256 * i + 256], p[rows, 512 + 32 * i : 544 + 32 * i]], axis=1))
        stack = jnp.concatenate([one, one, two, one, two, three], axis=0).T.astype(BF16)
        for k in range(3):
            cut = slice(96 * k, 96 * k + 96)
            decoded = lax.dot_general(stack[cut], lstack[i], (((1,), (0,)), ((), ())), preferred_element_type=F32)
            err[i, cut, :] = corr[cut, :] - decoded
            weight[i, cut, :] = ut[cut, :] - STEP * decoded
            span = pl.ds(96 * k, 96)
            store(err.at[i, span, :], e_new.at[span, :], out_sem.at[0, i, k])
            store(weight.at[i, span, :], w_new.at[span, :], out_sem.at[1, i, k])
    for d in loads:
        d.wait()
    mine = dot(own_left[...], p[...], 1, 0)[0:18]
    for i, (moment, m_new) in enumerate(((qmv, qm_new), (omv, om_new))):
        moment[:, 0:256] = DECAY * moment[:, 0:256] + mine[:, 256 * i : 256 * i + 256]
        moment[:, 256:288] = DECAY * moment[:, 256:288] + mine[:, 512 + 32 * i : 544 + 32 * i]
        store(moment, m_new, sm_sem.at[i])
    gainv[...] = (norms[1] - STEP * norms[0])[0:18]
    store(gainv, gains, sm_sem.at[2])
    flat = iota((24, 128), 0) * 128 + iota((24, 128), 1) - 9 * (lax.axis_index("rep") * 4 + lax.axis_index("shard"))
    for k in range(9):
        nmom[k] = DECAY * nmv[k] + jnp.sum(jnp.where(flat == k, norms[0], 0.0))
    for d in stores:
        d.wait()


def per_device(qg, og, qe, oe, qb, ob, qm, om, qw, ow, ng, nm, nw):
    hbm = pl.BlockSpec(memory_space=pltpu.HBM)
    vmem = pl.BlockSpec(memory_space=pltpu.VMEM)
    smem = pl.BlockSpec(memory_space=pltpu.SMEM)
    sem = pltpu.SemaphoreType.DMA

    def buf(*shape):
        return pltpu.VMEM(shape, F32)

    def turned(array):
        return jnp.swapaxes(array, 1, 2)[0]

    out = jax.ShapeDtypeStruct
    passed = pl.pallas_call(
        communicate,
        out_shape=tuple([out((288, 1152), F32)] * 4)
        + (
            out((2, 192, 1152), BF16),
            out((64, 640), F32),
            out((24, 64), F32),
            out((2, 24, 128), F32),
        ),
        in_specs=[hbm] * 13,
        out_specs=tuple([vmem] * 8),
        scratch_shapes=[
            buf(2, 288, 1152),
            buf(32, 288),
            buf(32, 288),
            buf(18, 288),
            buf(18, 288),
            buf(18, 288),
            buf(18, 288),
            buf(1, 1, 2304),
            pltpu.SMEM((9,), F32),
            pltpu.SMEM((9,), F32),
            buf(5, 1152, 128),
            buf(5, 576, 128),
            buf(5, 2, 72, 128),
            buf(5, 4, 72, 128),
            buf(5, 2, 72, 128),
            buf(5, 144, 128),
            buf(5, 7, 16, 128),
            buf(5, 7, 8, 128),
            buf(24, 640),
            pltpu.VMEM((144, 640), BF16),
            buf(64, 64),
            buf(64, 640),
            buf(4, 64, 128),
            buf(8, 8, 128),
            buf(8, 8, 128),
            buf(8, 8, 128),
            buf(8, 8, 128),
            buf(24, 640),
            buf(8, 24, 640),
            buf(8, 144, 640),
            buf(1152, 640),
            buf(2, 4, 16, 128),
            buf(8, 16, 128),
            buf(8, 16, 128),
            buf(2, 8, 8, 384),
            buf(2, 8, 8, 384),
            buf(2, 8, 8, 384),
            buf(2, 8, 8, 384),
            buf(2, 32, 640),
            buf(8, 16, 128),
            buf(72, 128),
            buf(8, 72, 128),
            buf(1152, 128),
            sem((2, 6)),
            sem((9,)),
            sem((5,)), sem((5,)),
            sem, sem((2, 5)),
            sem((5,)), sem((5,)),
            sem, sem((5,)),
            sem, sem,
            sem, sem,
            sem, sem,
            sem, sem,
            sem, sem((4,)),
            sem, sem((4,)),
            sem, sem((2,)),
            sem((2,)), sem((2,)),
            sem, sem,
            sem, sem,
            sem((2,)), sem((2,)),
            sem((2,)), sem((2,)),
            sem((2,)), sem((2,)),
            sem, sem,
            sem, sem,
        ],
        compiler_params=pltpu.CompilerParams(collective_id=0, has_side_effects=True, vmem_limit_bytes=28 << 20),
        name="communicate",
    )(*[pltpu.with_memory_space_constraint(x, pltpu.HBM) for x in (turned(qg), turned(og), turned(qe), turned(oe), qb.T, ob.T, qm, om, qw, ow, ng, nm, nw)])

    qw_new, ow_new, qm_new, om_new, qe_new, oe_new, gains, nmom = pl.pallas_call(
        decode,
        out_shape=(
            out((288, 1152), F32),
            out((288, 1152), F32),
            out((18, 288), F32),
            out((18, 288), F32),
            out((288, 1152), F32),
            out((288, 1152), F32),
            out((18, 128), F32),
            out((9,), F32),
        ),
        in_specs=[vmem] * 8 + [hbm] * 3,
        out_specs=tuple([hbm] * 7) + (smem,),
        scratch_shapes=[
            buf(2, 288, 1152),
            buf(2, 288, 1152),
            buf(18, 288),
            buf(18, 288),
            buf(18, 128),
            pltpu.SMEM((9,), F32),
            sem((3,)),
            sem((2, 2, 3)),
            sem((3,)),
        ],
        compiler_params=pltpu.CompilerParams(vmem_limit_bytes=24 << 20),
        name="decode",
    )(*passed, qm, om, nm)

    def back(array):
        return array.T[None]

    return qw_new.T, ow_new.T, qm_new, om_new, back(qe_new), back(oe_new), gains.reshape(-1), nmom


def solution(mesh):
    return jax.shard_map(
        per_device,
        mesh=mesh,
        in_specs=(
            P("rep", None, "shard"),
            P("rep", None, "shard"),
            P("rep", None, "shard"),
            P("rep", None, "shard"),
            P("shard", None),
            P("shard", None),
            P("rep", "shard"),
            P("rep", "shard"),
            P("rep", "shard"),
            P("rep", "shard"),
            P("rep", "shard", None),
            P(("rep", "shard")),
            P(("rep", "shard")),
        ),
        out_specs=(
            P(None, "shard"),
            P(None, "shard"),
            P("rep", "shard"),
            P("rep", "shard"),
            P("rep", None, "shard"),
            P("rep", None, "shard"),
            P(),
            P(("rep", "shard")),
        ),
        check_vma=False,
    )
```
